32 devices in a mesh: guide: 2 (over core), seq: 4 (over y, x), fsdp: 4 (over z).
Axes of the slice: x: 2, y: 2, z: 4, core: 2. Of those that a mesh axis runs over, the one named last changes fastest.
Arguments:
- hidden: bfloat16 [2, 1536, 3072], P('guide', 'seq', 'fsdp'), may hold values from -6 to 6
- modulation: float32 [2, 1, 5, 3072], P('guide'), may hold values from -3 to 3
- in_weight: bfloat16 [3072, 21504], P(None, 'fsdp'), may hold values from -0.109375 to 0.109375
- query_gain: float32 [128], replicated, may hold values from 1 to 20
- key_gain: float32 [128], replicated, may hold values from 1 to 20
- out_weight: bfloat16 [15360, 3072], P('fsdp', 'guide'), may hold values from -0.046875 to 0.046875
- head_weight: bfloat16 [3072, 64], replicated, may hold values from -0.109375 to 0.109375
- latents: float32 [64, 1536], P(None, 'seq'), may hold values from -6 to 6
- step_size: float32 [1], replicated, may hold values from -0.6 to -0.15
- guidance: float32 [1], replicated, may hold values from 1.5 to 5
- text_len: int32 [1], replicated, may hold values from 64 to 512, as said below
- tile_map: int32 [12], replicated, may hold values from 0 to 11, each once
Outputs:
- hidden_out: bfloat16 [2, 1536, 3072], P('guide', 'seq', 'fsdp')
- next_latents: float32 [64, 1536], P('guide', 'seq')
- hidden_norm: float32 [2, 1], P('guide')
- head_peak: float32 [2, 1], P('guide')
The draws below stay inside these ranges and needn't reach their ends.
Inputs may be any that keep to these rules, and one draw needn't show every extreme that they name: `text_len`: some request has exactly 512. `tile_map`: each tile number once.
All inputs are finite; a program needn't handle non-finite values.
Results may differ from the reference program's by a relative error of at most 0.01.
Values may be sent and summed in bfloat16 or wider, within the bound.
A program may use at most 192 MiB of HBM per device.

```python
import math
import jax
import jax.numpy as jnp
from jax import lax

D = 3072
HEADS = 24
HD = 128
FF = 12288
CH = 64
TXT = 512
IMG = 1024
TILE = 128
TOKENS = 1536
REQ = 1
NTILES = 12
HG = 6
FFG = 3072
INW = 21504
OUTW = 15360
N_FSDP = 4


def gain_draw(key, salt):
    base = jnp.exp(jax.random.uniform(jax.random.fold_in(key, salt), (HD,), jnp.float32, 0.0, math.log(3.0)))
    return base.astype(jnp.float32)


def draw_query_gain(key, part):
    return gain_draw(key, 21)


def draw_key_gain(key, part):
    return gain_draw(key, 31)


def draw_text_len(key, part):
    counts = jax.random.randint(jax.random.fold_in(key, 1), (REQ,), max(1, TXT // 8), TXT + 1)
    chosen = jax.random.randint(jax.random.fold_in(key, 2), (), 0, REQ)
    return jnp.where(jnp.arange(REQ) == chosen, TXT, counts).astype(jnp.int32)


def block_scale(key, dims, cuts, low, largest):
    def one(axis_at, blocks):
        draws = jax.random.uniform(jax.random.fold_in(jax.random.fold_in(key, 6), axis_at), (blocks,), jnp.float32, low / len(cuts), largest / len(cuts))
        return jnp.repeat(jnp.exp(draws), dims[axis_at] // blocks).reshape((-1,) + (1,) * (len(dims) - axis_at - 1))

    level = one(*cuts[0])
    for cut in cuts[1:]:
        level = level * one(*cut)
    return level


def bell_draw(key, shape, scale, reach, cuts=(), held_as=jnp.bfloat16):
    array = scale * jax.random.normal(key, shape, jnp.float32)
    if cuts:
        array = array * block_scale(key, shape, cuts, -0.22, 0.18)
    return jnp.clip(array, -reach, reach).astype(held_as)


def setup_inputs(seed: int = 0) -> dict:
    splits = jax.random.split(jax.random.key(seed), 13)
    hidden = bell_draw(splits[0], (2, TOKENS, D), 1.0, 6.0, ((0, 2), (1, 4), (2, 4)))
    modulation = bell_draw(splits[1], (2, REQ, 5, D), 0.5, 3.0, ((0, 2),), jnp.float32)
    in_weight = bell_draw(splits[2], (D, INW), D ** -0.5, 0.109375, ((1, 4),))
    query_gain = draw_query_gain(jax.random.fold_in(splits[12], 71), 0)
    key_gain = draw_key_gain(jax.random.fold_in(splits[12], 71), 0)
    out_weight = bell_draw(splits[5], (OUTW, D), OUTW ** -0.5, 0.046875, ((0, 4), (1, 2)))
    head_weight = bell_draw(splits[6], (D, CH), D ** -0.5, 0.109375)
    latents = bell_draw(splits[7], (CH, TOKENS), 1.0, 6.0, ((1, 4),), jnp.float32)
    step_size = jnp.clip(jax.random.uniform(splits[8], (REQ,), jnp.float32, -0.6, -0.15), -0.6, -0.15)
    guidance = jnp.clip(jax.random.uniform(splits[9], (REQ,), jnp.float32, 1.5, 5.0), 1.5, 5.0)
    text_len = draw_text_len(jax.random.fold_in(splits[12], 71), 0)
    tile_map = jax.random.permutation(splits[11], NTILES).astype(jnp.int32)
    return dict(hidden=hidden, modulation=modulation, in_weight=in_weight, query_gain=query_gain, key_gain=key_gain, out_weight=out_weight, head_weight=head_weight, latents=latents, step_size=step_size, guidance=guidance, text_len=text_len, tile_map=tile_map)


def layer_norm(values):
    middle = lax.optimization_barrier(jnp.mean(values, axis=-1, keepdims=True))
    power = lax.optimization_barrier(jnp.mean(values * values, axis=-1, keepdims=True))
    return (values - middle) * lax.rsqrt(power - middle * middle + 1e-06)

def describe(tile_map, text_len):
    index = jnp.arange(TOKENS, dtype=jnp.int32)
    logical = tile_map[index // TILE] * TILE + index % TILE
    request = (logical // (TXT + IMG)).astype(jnp.int32)
    position = logical % (TXT + IMG)
    image = position >= TXT
    valid = image | (position < text_len[request])
    return (request, image, valid)

def head_rms(values, gain):
    scaled = values * lax.rsqrt(lax.optimization_barrier(jnp.mean(values * values, axis=-1, keepdims=True)) + 1e-06)
    return (scaled * gain).astype(jnp.bfloat16)

def one_half(hidden_half, modulation_half, in_weight, query_gain, key_gain, out_weight, head_weight, request, valid):
    keep = valid[:, None]
    x_rows = hidden_half * keep.astype(jnp.bfloat16)
    shift = modulation_half[:, 0, :][request]
    scale = modulation_half[:, 1, :][request]
    gate = modulation_half[:, 2, :][request]
    normed = layer_norm(x_rows.astype(jnp.float32))
    modded = ((1.0 + scale) * normed + shift).astype(jnp.bfloat16)
    projected = jnp.dot(modded, in_weight, preferred_element_type=jnp.float32)
    grouped = projected.reshape(TOKENS, N_FSDP, -1)
    span = HG * HD
    queries = head_rms(grouped[:, :, :span].reshape(TOKENS, HEADS, HD), query_gain)
    keys = head_rms(grouped[:, :, span:2 * span].reshape(TOKENS, HEADS, HD), key_gain)
    values = grouped[:, :, 2 * span:3 * span].reshape(TOKENS, HEADS, HD).astype(jnp.bfloat16)
    mlp_part = grouped[:, :, 3 * span:].reshape(TOKENS, FF)
    allowed = (request[:, None] == request[None, :]) & valid[None, :]
    factor = HD ** (-0.5)

    def attend(operands):
        query_head, key_head, value_head = operands
        scores = jnp.dot(query_head, key_head.T, preferred_element_type=jnp.float32) * factor
        scores = jnp.where(allowed, scores, -jnp.inf)
        top = lax.optimization_barrier(jnp.max(scores, axis=-1, keepdims=True))
        raised = jnp.exp(scores - top)
        total = lax.optimization_barrier(jnp.sum(raised, axis=-1, keepdims=True))
        summed = jnp.dot(raised.astype(jnp.bfloat16), value_head, preferred_element_type=jnp.float32)
        return (summed / total).astype(jnp.bfloat16)
    attended = lax.map(attend, (queries.transpose(1, 0, 2), keys.transpose(1, 0, 2), values.transpose(1, 0, 2)))
    attended = attended.transpose(1, 0, 2).reshape(TOKENS, N_FSDP, span)
    activated = jax.nn.gelu(mlp_part, approximate=True).astype(jnp.bfloat16).reshape(TOKENS, N_FSDP, FFG)
    branch = jnp.concatenate([attended, activated], axis=2).reshape(TOKENS, OUTW)
    mixed = jnp.dot(branch, out_weight, preferred_element_type=jnp.float32)
    updated = ((x_rows.astype(jnp.float32) + gate * mixed) * keep.astype(jnp.float32)).astype(jnp.bfloat16)
    head_shift = modulation_half[:, 3, :][request]
    head_scale = modulation_half[:, 4, :][request]
    final = ((1.0 + head_scale) * layer_norm(updated.astype(jnp.float32)) + head_shift).astype(jnp.bfloat16)
    velocity = jnp.dot(final, head_weight, preferred_element_type=jnp.float32)
    return (updated, velocity)

def reference(hidden, modulation, in_weight, query_gain, key_gain, out_weight, head_weight, latents, step_size, guidance, text_len, tile_map):
    request, image, valid = describe(tile_map, text_len)
    member = request[None, :] == jnp.arange(REQ, dtype=jnp.int32)[:, None]
    updates = []
    velocities = []
    norms = []
    peaks = []
    for half in range(2):
        updated, velocity = one_half(hidden[half], modulation[half], in_weight, query_gain, key_gain, out_weight, head_weight, request, valid)
        squares = lax.optimization_barrier(jnp.sum(jnp.square(updated.astype(jnp.float32)), axis=1))
        total = lax.optimization_barrier(jnp.sum(jnp.where(member & valid[None, :], squares[None, :], 0.0), axis=1))
        count = (IMG + text_len).astype(jnp.float32) * D
        norms.append(jnp.sqrt(total / count))
        picked = jnp.where((member & image[None, :])[:, :, None], velocity[None, :, :], -jnp.inf)
        peaks.append(lax.optimization_barrier(jnp.max(picked, axis=(1, 2))))
        updates.append(updated)
        velocities.append(velocity)
    guided = velocities[1] + guidance[request][:, None] * (velocities[0] - velocities[1])
    stepped = latents.T + step_size[request][:, None] * guided
    next_latents = jnp.where(image[:, None], stepped, 0.0).T
    return (jnp.stack(updates), next_latents, jnp.stack(norms), jnp.stack(peaks))
```

```python
import jax
import jax.numpy as jnp
from jax import lax
from jax.experimental import pallas as pl
from jax.experimental.pallas import tpu as pltpu
from jax.sharding import PartitionSpec as P

HD = 128
TXT = 512
IMG = 1024
TILE = 128


def swapped(block, axis, stride):
    count = lax.axis_size(axis)
    route = []
    for low in range(count):
        high = low | 1 << stride
        if high != low and high < count:
            route += [(low, high), (high, low)]
    return lax.ppermute(block, axis, route)


def layer_norm(values):
    middle = jnp.mean(values, axis=-1, keepdims=True)
    power = jnp.mean(values * values, axis=-1, keepdims=True)
    return (values - middle) * lax.rsqrt(power - middle * middle + 1e-06)


def describe(index, tile_map, text_len):
    tile_index = index // TILE
    numbers = jnp.arange(tile_map.shape[0], dtype=jnp.int32)
    picked = jnp.sum(
        jnp.where(tile_index[:, None] == numbers[None, :], tile_map[None, :], 0), axis=1
    )
    logical = picked * TILE + index % TILE
    request = logical // (TXT + IMG)
    position = logical % (TXT + IMG)
    image = position >= TXT
    slots = jnp.arange(text_len.shape[0], dtype=jnp.int32)
    length = jnp.sum(jnp.where(request[:, None] == slots[None, :], text_len[None, :], 0), axis=1)
    valid = image | (position < length)
    return (request, image, valid)


def head_rms(values, gain):
    row_count = values.shape[0]
    shaped = values.reshape(row_count, -1, HD)
    scaled = shaped * lax.rsqrt(jnp.mean(shaped * shaped, axis=-1, keepdims=True) + 1e-06) * gain
    return scaled.reshape(row_count, -1).astype(jnp.bfloat16)


def shards(
    hidden,
    modulation,
    in_weight,
    query_gain,
    key_gain,
    out_weight,
    head_weight,
    latents,
    step_size,
    guidance,
    text_len,
    tile_map,
):
    row_count = hidden.shape[1]
    local_width = hidden.shape[2]
    requests = text_len.shape[0]
    first_row = lax.axis_index("seq") * row_count
    my_request, my_image, my_valid = describe(
        first_row + jnp.arange(row_count, dtype=jnp.int32), tile_map, text_len
    )
    request_hot = (my_request[:, None] == jnp.arange(requests, dtype=jnp.int32)[None, :]).astype(
        jnp.float32
    )

    def lookup(which):
        return jnp.dot(request_hot, modulation[0, :, which, :], precision=lax.Precision.HIGHEST)

    feature_start = lax.axis_index("fsdp") * local_width
    keep = my_valid[:, None]
    x_rows = hidden[0] * keep.astype(jnp.bfloat16)
    whole = lax.all_gather(x_rows, "fsdp", axis=1, tiled=True)
    normed = layer_norm(whole.astype(jnp.float32))
    modded = ((1.0 + lookup(1)) * normed + lookup(0)).astype(jnp.bfloat16)
    col_width = in_weight.shape[1]
    projected = jnp.dot(modded, in_weight, preferred_element_type=jnp.float32)
    span = (col_width - out_weight.shape[0]) // 2
    head_count = span // HD
    queries = head_rms(projected[:, :span], query_gain)
    keys = head_rms(projected[:, span : 2 * span], key_gain)
    values = projected[:, 2 * span : 3 * span].astype(jnp.bfloat16)
    mlp_part = projected[:, 3 * span :]
    query_heads = queries.reshape(row_count, head_count, HD)
    factor = HD ** (-0.5)
    key_piece = lax.all_gather(keys, "seq", axis=0, tiled=True)
    value_piece = lax.all_gather(values, "seq", axis=0, tiled=True)
    width = key_piece.shape[0]
    key_request, key_image, key_valid = describe(
        jnp.arange(width, dtype=jnp.int32), tile_map, text_len
    )
    allowed = (my_request[:, None] == key_request[None, :]) & key_valid[None, :]
    run_max = jnp.full((head_count, row_count), -1e30, jnp.float32)
    key_heads = key_piece.reshape(width, head_count, HD)
    value_heads = value_piece.reshape(width, head_count, HD)
    scores = (
        jnp.einsum("qhd,khd->hqk", query_heads, key_heads, preferred_element_type=jnp.float32)
        * factor
    )
    scores = jnp.where(allowed[None, :, :], scores, -jnp.inf)
    new_max = jnp.maximum(run_max, jnp.max(scores, axis=-1))
    raised = jnp.exp(scores - new_max[:, :, None])
    new_total = jnp.sum(raised, axis=-1)
    added = jnp.einsum(
        "hqk,khd->hqd", raised.astype(jnp.bfloat16), value_heads, preferred_element_type=jnp.float32
    )
    attended = (
        (added / new_total[:, :, None])
        .transpose(1, 0, 2)
        .reshape(row_count, span)
        .astype(jnp.bfloat16)
    )
    activated = jax.nn.gelu(mlp_part, approximate=True).astype(jnp.bfloat16)
    branch = jnp.concatenate([attended, activated], axis=1)
    terms = jnp.dot(
        branch,
        lax.all_gather(out_weight, "guide", axis=1, tiled=True),
        preferred_element_type=jnp.float32,
    )
    mixed = lax.psum_scatter(terms, "fsdp", scatter_dimension=1, tiled=True)
    gate = lax.dynamic_slice_in_dim(lookup(2), feature_start, local_width, 1)
    updated = ((x_rows.astype(jnp.float32) + gate * mixed) * keep.astype(jnp.float32)).astype(
        jnp.bfloat16
    )
    up_values = updated.astype(jnp.float32)
    contract = (((0,), (1,)), ((), ()))
    full_width = local_width * lax.axis_size("fsdp")
    row_sums, row_squares = lax.psum(
        (jnp.sum(up_values, axis=1), jnp.sum(up_values * up_values, axis=1)), "fsdp"
    )
    middle = (row_sums / full_width)[:, None]
    power = (row_squares / full_width)[:, None]
    local_normed = (up_values - middle) * lax.rsqrt(power - middle * middle + 1e-06)
    head_scale = lax.dynamic_slice_in_dim(lookup(4), feature_start, local_width, 1)
    head_shift = lax.dynamic_slice_in_dim(lookup(3), feature_start, local_width, 1)
    final = ((1.0 + head_scale) * local_normed + head_shift).astype(jnp.bfloat16)
    head_rows = lax.dynamic_slice_in_dim(head_weight, feature_start, local_width, 0)
    head_part = lax.dot_general(head_rows, final, contract, preferred_element_type=jnp.float32)
    velocity = lax.psum(head_part, "fsdp")
    partner = swapped(velocity.astype(jnp.bfloat16), "guide", 0).astype(velocity.dtype)
    is_first = lax.axis_index("guide") == 0
    cond_velocity = jnp.where(is_first, velocity, partner)
    uncond_velocity = jnp.where(is_first, partner, velocity)
    guide_rows = jnp.dot(request_hot, guidance, precision=lax.Precision.HIGHEST)
    step_rows = jnp.dot(request_hot, step_size, precision=lax.Precision.HIGHEST)
    guided = uncond_velocity + guide_rows[None, :] * (cond_velocity - uncond_velocity)
    channel_count = latents.shape[0] // lax.axis_size("guide")
    channel_start = lax.axis_index("guide") * channel_count
    my_guided = lax.dynamic_slice_in_dim(guided, channel_start, channel_count, 0)
    my_latents = lax.dynamic_slice_in_dim(latents, channel_start, channel_count, 0)
    next_latents = jnp.where(my_image[None, :], my_latents + step_rows[None, :] * my_guided, 0.0)
    member = my_request[None, :] == jnp.arange(requests, dtype=jnp.int32)[:, None]
    squares = jnp.sum(up_values * up_values, axis=1)
    local_total = jnp.sum(jnp.where(member & my_valid[None, :], squares[None, :], 0.0), axis=1)
    picked = jnp.where((member & my_image[None, :])[:, None, :], velocity[None, :, :], -jnp.inf)
    local_peak = jnp.max(picked, axis=(1, 2))
    total = lax.psum(local_total, ("seq", "fsdp"))
    peak = lax.pmax(local_peak, "seq")
    count = (IMG + text_len).astype(jnp.float32) * (local_width * lax.axis_size("fsdp"))
    hidden_norm = jnp.sqrt(total / count)
    return (updated[None], next_latents, hidden_norm[None], peak[None])


MESH = pl.DeviceIdType.MESH
BF = jnp.bfloat16
F32 = jnp.float32


def greet(axes):
    barrier = pltpu.get_barrier_semaphore()
    count = 0
    for axis in axes:
        size = lax.axis_size(axis)
        me = lax.axis_index(axis)
        for step in range(1, size):
            pl.semaphore_signal(
                barrier, inc=1, device_id={axis: lax.rem(me + step, size)}, device_id_type=MESH
            )
        count += size - 1
    pl.semaphore_wait(barrier, count)


def push(src, dst, send, recv, axis, target):
    return pltpu.make_async_remote_copy(
        src_ref=src,
        dst_ref=dst,
        send_sem=send,
        recv_sem=recv,
        device_id={axis: target},
        device_id_type=MESH,
    )


def spread(buf, send, recv, axis):
    size = lax.axis_size(axis)
    me = lax.axis_index(axis)
    copies = [
        push(buf.at[me], buf.at[me], send.at[s - 1], recv.at[me], axis, lax.rem(me + s, size))
        for s in range(1, size)
    ]
    for copy in copies:
        copy.start()
    return copies


def collect(buf, send, recv, axis, copies):
    size = lax.axis_size(axis)
    me = lax.axis_index(axis)
    for copy in copies:
        copy.wait_send()
    for s in range(1, size):
        other = lax.rem(me + s, size)
        push(buf.at[other], buf.at[other], send.at[s - 1], recv.at[other], axis, other).wait_recv()


def pack_stats(sums, squares):
    rows = sums.shape[0]
    lane = lax.broadcasted_iota(jnp.int32, (rows, 128), 1)
    both = jnp.where(lane == 0, sums, jnp.where(lane == 1, squares, 0.0))
    return jnp.transpose(both)[:8]


def open_stats(total, width):
    rows = total.shape[1]
    tall = jnp.concatenate([total, jnp.zeros((120, rows), F32)], axis=0)
    back = jnp.transpose(tall)
    middle = back[:, 0:1] / width
    power = back[:, 1:2] / width
    return middle, lax.rsqrt(power - middle * middle + 1e-06)


def pick(z, values):
    out = values[-1]
    for i in range(len(values) - 2, -1, -1):
        out = jnp.where(z == i, values[i], out)
    return out


def front_kernel(
    hid, keep, ss, qg, kg, w, q_out, k_out, v_out, act_out,
    xg, st, acc, wbuf, mod, xs, xr, ts, tr, ws,
):
    z = lax.axis_index("fsdp")
    rows, part = hid.shape
    width = part * 4
    span = q_out.shape[1]
    tiles = acc.shape[1] // span
    order = [
        z,
        pick(z, [1, 0, 3, 2]),
        pick(z, [2, 2, 1, 1]),
        pick(z, [3, 3, 0, 0]),
    ]

    def wcopy(p):
        at = pl.multiple_of(order[p] * part, part)
        return pltpu.make_async_copy(w.at[pl.ds(at, part), :], wbuf.at[p], ws.at[p])

    for p in range(4):
        wcopy(p).start()
    greet(("fsdp",))
    xg[z] = hid[...]

    def hop(c, way):
        target = jnp.minimum(z + 1, 3) if way == 0 else jnp.maximum(z - 1, 0)
        return push(xg.at[c], xg.at[c], xs.at[way, c], xr.at[c], "fsdp", target)

    @pl.when(z < 3)
    def _():
        hop(z, 0).start()

    @pl.when(z > 0)
    def _():
        hop(z, 1).start()

    own = (hid[...].astype(F32)) * keep[...]
    st[z] = pack_stats(
        jnp.sum(own, axis=1, keepdims=True), jnp.sum(own * own, axis=1, keepdims=True)
    )
    sent = spread(st, ts, tr, "fsdp")
    collect(st, ts, tr, "fsdp", sent)
    middle, inv = open_stats(st[0] + st[1] + st[2] + st[3], width)

    def arrive(c):
        hop(c, 0).wait_recv()

        @pl.when((c < z) & (z < 3))
        def _():
            hop(c, 0).start()

        @pl.when((c > z) & (z > 0))
        def _():
            hop(c, 1).start()

    inner = (z > 0) & (z < 3)
    for p in range(4):
        c = order[p]
        if p == 1:
            arrive(c)

            @pl.when(inner)
            def _():
                arrive(order[2])
        if p == 2:
            @pl.when(jnp.logical_not(inner))
            def _():
                arrive(order[2])
        if p == 3:
            arrive(c)
        vals = xg[c].astype(F32) * keep[...]
        both = ss[c]
        mod[...] = ((1.0 + both[1:2]) * ((vals - middle) * inv) + both[0:1]).astype(BF)
        wcopy(p).wait()

        def tile(i, carry):
            at = pl.ds(pl.multiple_of(i * span, span), span)
            got = jnp.dot(mod[...], wbuf[p, :, at], preferred_element_type=F32)
            if p == 0:
                acc[:, at] = got
            else:
                acc[:, at] += got
            return carry

        lax.fori_loop(0, tiles, tile, 0)

    def rms(src, gain, dst):
        for h in range(span // HD):
            at = slice(h * HD, (h + 1) * HD)
            vals = src[:, at]
            scaled = vals * lax.rsqrt(jnp.mean(vals * vals, axis=1, keepdims=True) + 1e-06)
            dst[:, at] = (scaled * gain[...]).astype(BF)

    rms(acc.at[:, pl.ds(0, span)], qg, q_out)
    rms(acc.at[:, pl.ds(span, span)], kg, k_out)
    v_out[...] = acc[:, pl.ds(2 * span, span)].astype(BF)

    def gelu(i, carry):
        frm = pl.ds(pl.multiple_of(3 * span + i * 256, 256), 256)
        to = pl.ds(pl.multiple_of(i * 256, 256), 256)
        act_out[:, to] = jax.nn.gelu(acc[:, frm], approximate=True).astype(BF)
        return carry

    lax.fori_loop(0, act_out.shape[1] // 256, gelu, 0)
    for c in range(4):
        @pl.when((z < 3) & (z >= c))
        def _():
            hop(c, 0).wait_send()

        @pl.when((z > 0) & (z <= c))
        def _():
            hop(c, 1).wait_send()


def vmem(count):
    return [pl.BlockSpec(memory_space=pltpu.VMEM)] * count


def front(hid, keep, ss, qg, kg, w, span):
    rows, part = hid.shape
    cols = w.shape[1]
    dma = pltpu.SemaphoreType.DMA
    shape = jax.ShapeDtypeStruct
    return pl.pallas_call(
        front_kernel,
        out_shape=(
            shape((rows, span), BF),
            shape((rows, span), BF),
            shape((rows, span), BF),
            shape((rows, cols - 3 * span), BF),
        ),
        in_specs=vmem(5) + [pl.BlockSpec(memory_space=pltpu.HBM)],
        out_specs=tuple(vmem(4)),
        scratch_shapes=[
            pltpu.VMEM((4, rows, part), BF),
            pltpu.VMEM((4, 8, rows), F32),
            pltpu.VMEM((rows, cols), F32),
            pltpu.VMEM((4, part, cols), BF),
            pltpu.VMEM((rows, part), BF),
            dma((2, 4)),
            dma((4,)),
            dma((3,)),
            dma((4,)),
            dma((4,)),
        ],
        compiler_params=pltpu.CompilerParams(
            collective_id=1, has_side_effects=True, vmem_limit_bytes=60 << 20
        ),
        cost_estimate=pl.CostEstimate(
            flops=2 * rows * 4 * part * cols, bytes_accessed=8 * part * cols, transcendentals=0
        ),
    )(hid, keep, ss, qg, kg, w)


def back_kernel(
    branch, hid, keep, flags, mine, hrows, lats, consts, w, up_out, lat_out, norm_out, peak_out,
    part, sbuf, rbuf, wbuf, st, vel, mix, swap, tot,
    ss, rs, ws, ts, tr, vs, vr, gs, gr, ks, kr,
):
    z = lax.axis_index("fsdp")
    g = lax.axis_index("guide")
    me = lax.axis_index("seq")
    rows, width = hid.shape
    order = [
        pick(z, [3, 3, 0, 0]),
        pick(z, [2, 0, 3, 1]),
        pick(z, [1, 2, 1, 2]),
        z,
    ]

    def wcopy(p):
        at = pl.multiple_of(order[p] * width, width)
        return pltpu.make_async_copy(w.at[:, pl.ds(at, width)], wbuf.at[p], ws.at[p])

    for p in range(4):
        wcopy(p).start()
    greet(("fsdp", "seq", "guide"))

    def hop(d, way):
        target = jnp.minimum(z + 1, 3) if way == 0 else jnp.maximum(z - 1, 0)
        return push(sbuf.at[d], rbuf.at[way, d], ss.at[d], rs.at[way, d], "fsdp", target)

    ends = (z == 0) | (z == 3)
    for p in range(4):
        d = order[p]
        wcopy(p).wait()

        def tile(i, carry):
            at = pl.ds(pl.multiple_of(i * 256, 256), 256)
            part[d, :, at] = jnp.dot(branch[...], wbuf[p, :, at], preferred_element_type=F32)
            return carry

        lax.fori_loop(0, width // 256, tile, 0)
        if p < 3:
            @pl.when(z == 0)
            def _():
                sbuf[d] = part[d].astype(BF)
                hop(d, 0).start()

            @pl.when(z == 3)
            def _():
                sbuf[d] = part[d].astype(BF)
                hop(d, 1).start()

    def relay(d, way):
        hop(d, way).wait_recv()
        sbuf[d] = (part[d] + rbuf[way, d].astype(F32)).astype(BF)
        hop(d, way).start()

    @pl.when(z == 1)
    def _():
        relay(3, 0)
        relay(2, 0)
        relay(0, 1)

    @pl.when(z == 2)
    def _():
        relay(0, 1)
        relay(1, 1)
        relay(3, 0)

    mix[...] = part[z]

    @pl.when(z > 0)
    def _():
        hop(z, 0).wait_recv()
        mix[...] += rbuf[0, z].astype(F32)

    @pl.when(z < 3)
    def _():
        hop(z, 1).wait_recv()
        mix[...] += rbuf[1, z].astype(F32)

    x = hid[...].astype(F32) * keep[...]
    up = ((x + mine[0:1] * mix[...]) * keep[...]).astype(BF)
    up_out[...] = up
    wide = up.astype(F32)
    st[z] = pack_stats(
        jnp.sum(wide, axis=1, keepdims=True), jnp.sum(wide * wide, axis=1, keepdims=True)
    )
    sent = spread(st, ts, tr, "fsdp")
    collect(st, ts, tr, "fsdp", sent)
    total = st[0] + st[1] + st[2] + st[3]
    middle, inv = open_stats(total, width * 4)
    final = ((1.0 + mine[2:3]) * ((wide - middle) * inv) + mine[1:2]).astype(BF)
    vel[z] = lax.dot_general(
        hrows[...], final, (((1,), (1,)), ((), ())), preferred_element_type=F32
    )
    sent = spread(vel, vs, vr, "fsdp")
    collect(vel, vs, vr, "fsdp", sent)
    mix[pl.ds(0, 64), pl.ds(0, rows)] = vel[0] + vel[1] + vel[2] + vel[3]
    velocity = mix[pl.ds(0, 64), pl.ds(0, rows)]
    half = lats.shape[0]
    other = 1 - g
    swap[0] = mix[pl.ds(pl.multiple_of(other * half, half), half), pl.ds(0, rows)]
    cross = push(swap.at[0], swap.at[1], gs, gr, "guide", other)
    cross.start()
    full = jnp.sum(jnp.where(flags[0:1] > 0.0, total[1:2], 0.0), axis=1, keepdims=True)
    top = jnp.max(jnp.where(flags[1:2] > 0.0, velocity, -jnp.inf), axis=1, keepdims=True)
    top = jnp.max(top, axis=0, keepdims=True)
    line = lax.broadcasted_iota(jnp.int32, (8, 128), 0)
    tot[me] = jnp.where(line == 0, full, top)
    sent = spread(tot, ks, kr, "seq")
    collect(tot, ks, kr, "seq", sent)
    added = tot[0] + tot[1] + tot[2] + tot[3]
    peak = jnp.maximum(jnp.maximum(tot[0], tot[1]), jnp.maximum(tot[2], tot[3]))
    norm_out[...] = jnp.sqrt(added[0:1, 0:1] / consts[0:1, 2:3])
    peak_out[...] = peak[1:2, 0:1]
    cross.wait()
    own = mix[pl.ds(pl.multiple_of(g * half, half), half), pl.ds(0, rows)]
    theirs = swap[1]
    cond = jnp.where(g == 0, own, theirs)
    free = jnp.where(g == 0, theirs, own)
    guided = free + consts[0:1, 0:1] * (cond - free)
    lat_out[...] = jnp.where(flags[1:2] > 0.0, lats[...] + consts[0:1, 1:2] * guided, 0.0)
    for d in range(4):
        @pl.when(z != d)
        def _():
            hop(d, 0).wait_send()


def back(branch, hid, keep, flags, mine, hrows, lats, consts, w):
    rows, width = hid.shape
    depth = w.shape[0]
    dma = pltpu.SemaphoreType.DMA
    shape = jax.ShapeDtypeStruct
    return pl.pallas_call(
        back_kernel,
        out_shape=(
            shape((rows, width), BF),
            shape(lats.shape, F32),
            shape((1, 1), F32),
            shape((1, 1), F32),
        ),
        in_specs=vmem(8) + [pl.BlockSpec(memory_space=pltpu.HBM)],
        out_specs=tuple(vmem(4)),
        scratch_shapes=[
            pltpu.VMEM((4, rows, width), F32),
            pltpu.VMEM((4, rows, width), BF),
            pltpu.VMEM((2, 4, rows, width), BF),
            pltpu.VMEM((4, depth, width), BF),
            pltpu.VMEM((4, 8, rows), F32),
            pltpu.VMEM((4, 64, rows), F32),
            pltpu.VMEM((rows, width), F32),
            pltpu.VMEM((2, lats.shape[0], rows), F32),
            pltpu.VMEM((4, 8, 128), F32),
            dma((4,)),
            dma((2, 4)),
            dma((4,)),
            dma((3,)),
            dma((4,)),
            dma((3,)),
            dma((4,)),
            dma,
            dma,
            dma((3,)),
            dma((4,)),
        ],
        compiler_params=pltpu.CompilerParams(
            collective_id=2, has_side_effects=True, vmem_limit_bytes=60 << 20
        ),
        cost_estimate=pl.CostEstimate(
            flops=8 * rows * depth * width, bytes_accessed=8 * depth * width, transcendentals=0
        ),
    )(branch, hid, keep, flags, mine, hrows, lats, consts, w)


def fast_shards(
    hidden,
    modulation,
    in_weight,
    query_gain,
    key_gain,
    out_weight,
    head_weight,
    latents,
    step_size,
    guidance,
    text_len,
    tile_map,
):
    row_count, local_width = hidden.shape[1:]
    whole_out = lax.all_gather(out_weight, "guide", axis=1, tiled=True)
    first_row = lax.axis_index("seq") * row_count
    _, my_image, my_valid = describe(
        first_row + jnp.arange(row_count, dtype=jnp.int32), tile_map, text_len
    )
    keep = my_valid.astype(F32)[:, None]
    span = (in_weight.shape[1] - out_weight.shape[0]) // 2
    ss = modulation[0, 0, :2].reshape(2, 4, local_width).transpose(1, 0, 2)
    queries, keys, values, activated = front(
        hidden[0], keep, ss, query_gain[None], key_gain[None], in_weight, span
    )
    flags = jnp.concatenate(
        [my_valid.astype(F32)[None], my_image.astype(F32)[None], jnp.zeros((6, row_count), F32)]
    )
    start = lax.axis_index("fsdp") * local_width
    mine = lax.dynamic_slice_in_dim(modulation[0, 0, 2:], start, local_width, 1)
    head_rows = lax.dynamic_slice_in_dim(head_weight, start, local_width, 0).T
    channels = latents.shape[0] // 2
    my_latents = lax.dynamic_slice_in_dim(
        latents, lax.axis_index("guide") * channels, channels, 0
    )
    count = (IMG + text_len).astype(F32) * (local_width * 4)
    consts = jnp.concatenate([guidance, step_size, count, jnp.zeros((125,), F32)])[None]
    head_count = span // HD
    key_piece = lax.all_gather(keys, "seq", axis=0, tiled=True)
    value_piece = lax.all_gather(values, "seq", axis=0, tiled=True)
    tokens = key_piece.shape[0]
    _, _, key_valid = describe(jnp.arange(tokens, dtype=jnp.int32), tile_map, text_len)
    scores = jnp.einsum(
        "qhd,khd->hqk",
        queries.reshape(row_count, head_count, HD),
        key_piece.reshape(tokens, head_count, HD),
        preferred_element_type=F32,
    ) * (HD ** (-0.5))
    scores = jnp.where(key_valid[None, None, :], scores, -jnp.inf)
    raised = jnp.exp(scores - jnp.max(scores, axis=-1, keepdims=True))
    weight_sum = jnp.sum(raised, axis=-1)
    added = jnp.einsum(
        "hqk,khd->hqd",
        raised.astype(BF),
        value_piece.reshape(tokens, head_count, HD),
        preferred_element_type=F32,
    )
    attended = (
        (added / weight_sum[:, :, None]).transpose(1, 0, 2).reshape(row_count, span).astype(BF)
    )
    branch = jnp.concatenate([attended, activated], axis=1)
    updated, next_latents, norm, peak = back(
        branch, hidden[0], keep, flags, mine, head_rows, my_latents, consts, whole_out
    )
    return (updated[None], next_latents, norm, peak)


def solution(mesh):
    placed = (
        P("guide", "seq", "fsdp"),
        P("guide", None, None, None),
        P(None, "fsdp"),
        P(),
        P(),
        P("fsdp", "guide"),
        P(),
        P(None, "seq"),
        P(),
        P(),
        P(),
        P(),
    )
    shape = dict(mesh.shape)
    planned = shape["fsdp"] == 4 and shape["seq"] == 4 and shape["guide"] == 2
    return jax.shard_map(
        fast_shards if planned else shards,
        mesh=mesh,
        in_specs=placed,
        out_specs=(
            P("guide", "seq", "fsdp"),
            P("guide", "seq"),
            P("guide", None),
            P("guide", None),
        ),
        check_vma=False,
    )
```

```python
import jax
import jax.numpy as jnp
from jax import lax
from jax.experimental import pallas as pl
from jax.experimental.pallas import tpu as pltpu
from jax.sharding import PartitionSpec as P

HD = 128
TXT = 512
IMG = 1024
TILE = 128


def swapped(block, axis, stride):
    count = lax.axis_size(axis)
    route = []
    for low in range(count):
        high = low | 1 << stride
        if high != low and high < count:
            route += [(low, high), (high, low)]
    return lax.ppermute(block, axis, route)


def layer_norm(values):
    middle = jnp.mean(values, axis=-1, keepdims=True)
    power = jnp.mean(values * values, axis=-1, keepdims=True)
    return (values - middle) * lax.rsqrt(power - middle * middle + 1e-06)


def describe(index, tile_map, text_len):
    tile_index = index // TILE
    numbers = jnp.arange(tile_map.shape[0], dtype=jnp.int32)
    picked = jnp.sum(
        jnp.where(tile_index[:, None] == numbers[None, :], tile_map[None, :], 0), axis=1
    )
    logical = picked * TILE + index % TILE
    request = logical // (TXT + IMG)
    position = logical % (TXT + IMG)
    image = position >= TXT
    slots = jnp.arange(text_len.shape[0], dtype=jnp.int32)
    length = jnp.sum(jnp.where(request[:, None] == slots[None, :], text_len[None, :], 0), axis=1)
    valid = image | (position < length)
    return (request, image, valid)


def head_rms(values, gain):
    row_count = values.shape[0]
    shaped = values.reshape(row_count, -1, HD)
    scaled = shaped * lax.rsqrt(jnp.mean(shaped * shaped, axis=-1, keepdims=True) + 1e-06) * gain
    return scaled.reshape(row_count, -1).astype(jnp.bfloat16)


def shards(
    hidden,
    modulation,
    in_weight,
    query_gain,
    key_gain,
    out_weight,
    head_weight,
    latents,
    step_size,
    guidance,
    text_len,
    tile_map,
):
    row_count = hidden.shape[1]
    local_width = hidden.shape[2]
    requests = text_len.shape[0]
    first_row = lax.axis_index("seq") * row_count
    my_request, my_image, my_valid = describe(
        first_row + jnp.arange(row_count, dtype=jnp.int32), tile_map, text_len
    )
    request_hot = (my_request[:, None] == jnp.arange(requests, dtype=jnp.int32)[None, :]).astype(
        jnp.float32
    )

    def lookup(which):
        return jnp.dot(request_hot, modulation[0, :, which, :], precision=lax.Precision.HIGHEST)

    feature_start = lax.axis_index("fsdp") * local_width
    keep = my_valid[:, None]
    x_rows = hidden[0] * keep.astype(jnp.bfloat16)
    whole = lax.all_gather(x_rows, "fsdp", axis=1, tiled=True)
    normed = layer_norm(whole.astype(jnp.float32))
    modded = ((1.0 + lookup(1)) * normed + lookup(0)).astype(jnp.bfloat16)
    col_width = in_weight.shape[1]
    projected = jnp.dot(modded, in_weight, preferred_element_type=jnp.float32)
    span = (col_width - out_weight.shape[0]) // 2
    head_count = span // HD
    queries = head_rms(projected[:, :span], query_gain)
    keys = head_rms(projected[:, span : 2 * span], key_gain)
    values = projected[:, 2 * span : 3 * span].astype(jnp.bfloat16)
    mlp_part = projected[:, 3 * span :]
    query_heads = queries.reshape(row_count, head_count, HD)
    factor = HD ** (-0.5)
    key_piece = lax.all_gather(keys, "seq", axis=0, tiled=True)
    value_piece = lax.all_gather(values, "seq", axis=0, tiled=True)
    width = key_piece.shape[0]
    key_request, key_image, key_valid = describe(
        jnp.arange(width, dtype=jnp.int32), tile_map, text_len
    )
    allowed = (my_request[:, None] == key_request[None, :]) & key_valid[None, :]
    run_max = jnp.full((head_count, row_count), -1e30, jnp.float32)
    key_heads = key_piece.reshape(width, head_count, HD)
    value_heads = value_piece.reshape(width, head_count, HD)
    scores = (
        jnp.einsum("qhd,khd->hqk", query_heads, key_heads, preferred_element_type=jnp.float32)
        * factor
    )
    scores = jnp.where(allowed[None, :, :], scores, -jnp.inf)
    new_max = jnp.maximum(run_max, jnp.max(scores, axis=-1))
    raised = jnp.exp(scores - new_max[:, :, None])
    new_total = jnp.sum(raised, axis=-1)
    added = jnp.einsum(
        "hqk,khd->hqd", raised.astype(jnp.bfloat16), value_heads, preferred_element_type=jnp.float32
    )
    attended = (
        (added / new_total[:, :, None])
        .transpose(1, 0, 2)
        .reshape(row_count, span)
        .astype(jnp.bfloat16)
    )
    activated = jax.nn.gelu(mlp_part, approximate=True).astype(jnp.bfloat16)
    branch = jnp.concatenate([attended, activated], axis=1)
    terms = jnp.dot(
        branch,
        lax.all_gather(out_weight, "guide", axis=1, tiled=True),
        preferred_element_type=jnp.float32,
    )
    mixed = lax.psum_scatter(terms, "fsdp", scatter_dimension=1, tiled=True)
    gate = lax.dynamic_slice_in_dim(lookup(2), feature_start, local_width, 1)
    updated = ((x_rows.astype(jnp.float32) + gate * mixed) * keep.astype(jnp.float32)).astype(
        jnp.bfloat16
    )
    up_values = updated.astype(jnp.float32)
    contract = (((0,), (1,)), ((), ()))
    full_width = local_width * lax.axis_size("fsdp")
    row_sums, row_squares = lax.psum(
        (jnp.sum(up_values, axis=1), jnp.sum(up_values * up_values, axis=1)), "fsdp"
    )
    middle = (row_sums / full_width)[:, None]
    power = (row_squares / full_width)[:, None]
    local_normed = (up_values - middle) * lax.rsqrt(power - middle * middle + 1e-06)
    head_scale = lax.dynamic_slice_in_dim(lookup(4), feature_start, local_width, 1)
    head_shift = lax.dynamic_slice_in_dim(lookup(3), feature_start, local_width, 1)
    final = ((1.0 + head_scale) * local_normed + head_shift).astype(jnp.bfloat16)
    head_rows = lax.dynamic_slice_in_dim(head_weight, feature_start, local_width, 0)
    head_part = lax.dot_general(head_rows, final, contract, preferred_element_type=jnp.float32)
    velocity = lax.psum(head_part, "fsdp")
    partner = swapped(velocity.astype(jnp.bfloat16), "guide", 0).astype(velocity.dtype)
    is_first = lax.axis_index("guide") == 0
    cond_velocity = jnp.where(is_first, velocity, partner)
    uncond_velocity = jnp.where(is_first, partner, velocity)
    guide_rows = jnp.dot(request_hot, guidance, precision=lax.Precision.HIGHEST)
    step_rows = jnp.dot(request_hot, step_size, precision=lax.Precision.HIGHEST)
    guided = uncond_velocity + guide_rows[None, :] * (cond_velocity - uncond_velocity)
    channel_count = latents.shape[0] // lax.axis_size("guide")
    channel_start = lax.axis_index("guide") * channel_count
    my_guided = lax.dynamic_slice_in_dim(guided, channel_start, channel_count, 0)
    my_latents = lax.dynamic_slice_in_dim(latents, channel_start, channel_count, 0)
    next_latents = jnp.where(my_image[None, :], my_latents + step_rows[None, :] * my_guided, 0.0)
    member = my_request[None, :] == jnp.arange(requests, dtype=jnp.int32)[:, None]
    squares = jnp.sum(up_values * up_values, axis=1)
    local_total = jnp.sum(jnp.where(member & my_valid[None, :], squares[None, :], 0.0), axis=1)
    picked = jnp.where((member & my_image[None, :])[:, None, :], velocity[None, :, :], -jnp.inf)
    local_peak = jnp.max(picked, axis=(1, 2))
    total = lax.psum(local_total, ("seq", "fsdp"))
    peak = lax.pmax(local_peak, "seq")
    count = (IMG + text_len).astype(jnp.float32) * (local_width * lax.axis_size("fsdp"))
    hidden_norm = jnp.sqrt(total / count)
    return (updated[None], next_latents, hidden_norm[None], peak[None])


MESH = pl.DeviceIdType.MESH
BF = jnp.bfloat16
F32 = jnp.float32


def greet(axes):
    barrier = pltpu.get_barrier_semaphore()
    count = 0
    for axis in axes:
        size = lax.axis_size(axis)
        me = lax.axis_index(axis)
        for step in range(1, size):
            pl.semaphore_signal(
                barrier, inc=1, device_id={axis: lax.rem(me + step, size)}, device_id_type=MESH
            )
        count += size - 1
    pl.semaphore_wait(barrier, count)


def push(src, dst, send, recv, axis, target):
    return pltpu.make_async_remote_copy(
        src_ref=src,
        dst_ref=dst,
        send_sem=send,
        recv_sem=recv,
        device_id={axis: target},
        device_id_type=MESH,
    )


def spread(buf, send, recv, axis):
    size = lax.axis_size(axis)
    me = lax.axis_index(axis)
    copies = [
        push(buf.at[me], buf.at[me], send.at[s - 1], recv.at[me], axis, lax.rem(me + s, size))
        for s in range(1, size)
    ]
    for copy in copies:
        copy.start()
    return copies


def collect(buf, send, recv, axis, copies):
    size = lax.axis_size(axis)
    me = lax.axis_index(axis)
    for copy in copies:
        copy.wait_send()
    for s in range(1, size):
        other = lax.rem(me + s, size)
        push(buf.at[other], buf.at[other], send.at[s - 1], recv.at[other], axis, other).wait_recv()


def pack_stats(sums, squares):
    rows = sums.shape[0]
    lane = lax.broadcasted_iota(jnp.int32, (rows, 128), 1)
    both = jnp.where(lane == 0, sums, jnp.where(lane == 1, squares, 0.0))
    return jnp.transpose(both)[:8]


def open_stats(total, width):
    rows = total.shape[1]
    tall = jnp.concatenate([total, jnp.zeros((120, rows), F32)], axis=0)
    back = jnp.transpose(tall)
    middle = back[:, 0:1] / width
    power = back[:, 1:2] / width
    return middle, lax.rsqrt(power - middle * middle + 1e-06)


def pick(z, values):
    out = values[-1]
    for i in range(len(values) - 2, -1, -1):
        out = jnp.where(z == i, values[i], out)
    return out


def front_kernel(
    hid, keep, ss, qg, kg, w, q_out, k_out, v_out, act_out,
    xg, st, acc, wbuf, mod, xs, xr, ts, tr, ws,
):
    z = lax.axis_index("fsdp")
    rows, part = hid.shape
    width = part * 4
    span = q_out.shape[1]
    tiles = acc.shape[1] // span
    order = [
        z,
        pick(z, [1, 0, 3, 2]),
        pick(z, [2, 2, 1, 1]),
        pick(z, [3, 3, 0, 0]),
    ]

    def wcopy(p):
        at = pl.multiple_of(order[p] * part, part)
        return pltpu.make_async_copy(w.at[pl.ds(at, part), :], wbuf.at[p], ws.at[p])

    for p in range(4):
        wcopy(p).start()
    greet(("fsdp",))
    xg[z] = hid[...]

    def hop(c, way):
        target = jnp.minimum(z + 1, 3) if way == 0 else jnp.maximum(z - 1, 0)
        return push(xg.at[c], xg.at[c], xs.at[way, c], xr.at[c], "fsdp", target)

    @pl.when(z < 3)
    def _():
        hop(z, 0).start()

    @pl.when(z > 0)
    def _():
        hop(z, 1).start()

    own = (hid[...].astype(F32)) * keep[...]
    st[z] = pack_stats(
        jnp.sum(own, axis=1, keepdims=True), jnp.sum(own * own, axis=1, keepdims=True)
    )
    sent = spread(st, ts, tr, "fsdp")
    collect(st, ts, tr, "fsdp", sent)
    middle, inv = open_stats(st[0] + st[1] + st[2] + st[3], width)

    def arrive(c):
        hop(c, 0).wait_recv()

        @pl.when((c < z) & (z < 3))
        def _():
            hop(c, 0).start()

        @pl.when((c > z) & (z > 0))
        def _():
            hop(c, 1).start()

    inner = (z > 0) & (z < 3)
    for p in range(4):
        c = order[p]
        if p == 1:
            arrive(c)

            @pl.when(inner)
            def _():
                arrive(order[2])
        if p == 2:
            @pl.when(jnp.logical_not(inner))
            def _():
                arrive(order[2])
        if p == 3:
            arrive(c)
        vals = xg[c].astype(F32) * keep[...]
        both = ss[c]
        mod[...] = ((1.0 + both[1:2]) * ((vals - middle) * inv) + both[0:1]).astype(BF)
        wcopy(p).wait()

        def tile(i, carry):
            at = pl.ds(pl.multiple_of(i * span, span), span)
            got = jnp.dot(mod[...], wbuf[p, :, at], preferred_element_type=F32)
            if p == 0:
                acc[:, at] = got
            else:
                acc[:, at] += got
            return carry

        lax.fori_loop(0, tiles, tile, 0)

    def rms(src, gain, dst):
        for h in range(span // HD):
            at = slice(h * HD, (h + 1) * HD)
            vals = src[:, at]
            scaled = vals * lax.rsqrt(jnp.mean(vals * vals, axis=1, keepdims=True) + 1e-06)
            dst[:, at] = (scaled * gain[...]).astype(BF)

    rms(acc.at[:, pl.ds(0, span)], qg, q_out)
    rms(acc.at[:, pl.ds(span, span)], kg, k_out)
    v_out[...] = acc[:, pl.ds(2 * span, span)].astype(BF)

    def gelu(i, carry):
        frm = pl.ds(pl.multiple_of(3 * span + i * 256, 256), 256)
        to = pl.ds(pl.multiple_of(i * 256, 256), 256)
        act_out[:, to] = jax.nn.gelu(acc[:, frm], approximate=True).astype(BF)
        return carry

    lax.fori_loop(0, act_out.shape[1] // 256, gelu, 0)
    for c in range(4):
        @pl.when((z < 3) & (z >= c))
        def _():
            hop(c, 0).wait_send()

        @pl.when((z > 0) & (z <= c))
        def _():
            hop(c, 1).wait_send()


def vmem(count):
    return [pl.BlockSpec(memory_space=pltpu.VMEM)] * count


def front(hid, keep, ss, qg, kg, w, span):
    rows, part = hid.shape
    cols = w.shape[1]
    dma = pltpu.SemaphoreType.DMA
    shape = jax.ShapeDtypeStruct
    return pl.pallas_call(
        front_kernel,
        out_shape=(
            shape((rows, span), BF),
            shape((rows, span), BF),
            shape((rows, span), BF),
            shape((rows, cols - 3 * span), BF),
        ),
        in_specs=vmem(5) + [pl.BlockSpec(memory_space=pltpu.HBM)],
        out_specs=tuple(vmem(4)),
        scratch_shapes=[
            pltpu.VMEM((4, rows, part), BF),
            pltpu.VMEM((4, 8, rows), F32),
            pltpu.VMEM((rows, cols), F32),
            pltpu.VMEM((4, part, cols), BF),
            pltpu.VMEM((rows, part), BF),
            dma((2, 4)),
            dma((4,)),
            dma((3,)),
            dma((4,)),
            dma((4,)),
        ],
        compiler_params=pltpu.CompilerParams(
            collective_id=1, has_side_effects=True, vmem_limit_bytes=60 << 20
        ),
        cost_estimate=pl.CostEstimate(
            flops=2 * rows * 4 * part * cols, bytes_accessed=8 * part * cols, transcendentals=0
        ),
    )(hid, keep, ss, qg, kg, w)


def back_kernel(
    q, k, v, act, kval, hid, keep, flags, mine, hrows, lats, consts, w,
    up_out, lat_out, norm_out, peak_out,
    kbuf, vbuf, high, low, gain, att, part, sbuf, rbuf, wbuf, st, vel, mix, swap, tot,
    ps, kq, vq, ss, rs, ws, ts, tr, vs, vr, gs, gr, ks, kr,
):
    z = lax.axis_index("fsdp")
    g = lax.axis_index("guide")
    me = lax.axis_index("seq")
    rows, width = hid.shape
    order = [
        pick(z, [3, 3, 0, 0]),
        pick(z, [2, 0, 3, 1]),
        pick(z, [1, 2, 1, 2]),
        z,
    ]

    def wcopy(p):
        at = pl.multiple_of(order[p] * width, width)
        return pltpu.make_async_copy(w.at[:, pl.ds(at, width)], wbuf.at[p], ws.at[p])

    for p in range(4):
        wcopy(p).start()
    kbuf[me] = k[...]
    vbuf[me] = v[...]
    greet(("fsdp", "seq", "guide"))
    near_x = me + 1 - 2 * lax.rem(me, 2)
    near_y = lax.rem(me + 2, 4)
    across = 3 - me

    def key_hop(src, at, target):
        return push(kbuf.at[src], kbuf.at[src], ps.at[at], kq.at[src], "seq", target)

    def value_hop(src, at, target):
        return push(vbuf.at[src], vbuf.at[src], ps.at[at], vq.at[src], "seq", target)

    moves = [
        key_hop(me, 0, near_x),
        value_hop(me, 1, near_y),
        key_hop(me, 2, near_y),
        value_hop(me, 3, near_x),
        key_hop(near_x, 4, near_y),
        value_hop(near_y, 5, near_x),
    ]
    for move in moves[:4]:
        move.start()

    span = q.shape[1]
    rate = HD ** (-0.5) * 1.4426950408889634

    def attend(src, first):
        open_keys = kval[src] > 0.0

        def heads(i, carry):
            for j in range(2):
                h = i * 2 + j
                at = pl.ds(pl.multiple_of(h * HD, HD), HD)
                s = lax.dot_general(
                    q[:, at],
                    kbuf[src, :, at],
                    (((1,), (1,)), ((), ())),
                    preferred_element_type=F32,
                )
                s = jnp.where(open_keys, s, -1e30)
                top = jnp.max(s, axis=1, keepdims=True)
                if not first:
                    top = jnp.maximum(top, high[h])
                p = jnp.exp2((s - top) * rate)
                total = jnp.sum(p, axis=1, keepdims=True)
                got = jnp.dot(p.astype(BF), vbuf[src, :, at], preferred_element_type=F32)
                if not first:
                    shrink = jnp.exp2((high[h] - top) * rate)
                    total = total + low[h] * shrink
                    got = got + gain[:, at] * shrink
                high[h] = top
                low[h] = total
                gain[:, at] = got
            return carry

        lax.fori_loop(0, span // (2 * HD), heads, 0)

    def hop(d, way):
        target = jnp.minimum(z + 1, 3) if way == 0 else jnp.maximum(z - 1, 0)
        return push(sbuf.at[d], rbuf.at[way, d], ss.at[d], rs.at[way, d], "fsdp", target)

    ends = (z == 0) | (z == 3)
    attend(me, True)
    for p in range(4):
        d = order[p]
        wcopy(p).wait()

        def tile(i, carry):
            at = pl.ds(pl.multiple_of(i * 256, 256), 256)
            part[d, :, at] = jnp.dot(act[...], wbuf[p, span:, at], preferred_element_type=F32)
            return carry

        lax.fori_loop(0, width // 256, tile, 0)
        if p == 2:
            key_hop(near_x, 0, near_x).wait_recv()
            moves[4].start()
            value_hop(near_y, 1, near_y).wait_recv()
            moves[5].start()
    value_hop(near_x, 3, near_x).wait_recv()
    attend(near_x, False)
    key_hop(near_y, 2, near_y).wait_recv()
    attend(near_y, False)
    key_hop(across, 4, near_y).wait_recv()
    value_hop(across, 5, near_x).wait_recv()
    attend(across, False)
    for h in range(span // HD):
        at = slice(h * HD, (h + 1) * HD)
        att[:, at] = (gain[:, at] / low[h]).astype(BF)
    for p in range(4):
        d = order[p]

        def tile(i, carry):
            at = pl.ds(pl.multiple_of(i * 256, 256), 256)
            part[d, :, at] += jnp.dot(att[...], wbuf[p, :span, at], preferred_element_type=F32)
            return carry

        lax.fori_loop(0, width // 256, tile, 0)
        if p < 3:
            @pl.when(z == 0)
            def _():
                sbuf[d] = part[d].astype(BF)
                hop(d, 0).start()

            @pl.when(z == 3)
            def _():
                sbuf[d] = part[d].astype(BF)
                hop(d, 1).start()

    def relay(d, way):
        hop(d, way).wait_recv()
        sbuf[d] = (part[d] + rbuf[way, d].astype(F32)).astype(BF)
        hop(d, way).start()

    @pl.when(z == 1)
    def _():
        relay(3, 0)
        relay(2, 0)
        relay(0, 1)

    @pl.when(z == 2)
    def _():
        relay(0, 1)
        relay(1, 1)
        relay(3, 0)

    mix[...] = part[z]

    @pl.when(z > 0)
    def _():
        hop(z, 0).wait_recv()
        mix[...] += rbuf[0, z].astype(F32)

    @pl.when(z < 3)
    def _():
        hop(z, 1).wait_recv()
        mix[...] += rbuf[1, z].astype(F32)

    x = hid[...].astype(F32) * keep[...]
    up = ((x + mine[0:1] * mix[...]) * keep[...]).astype(BF)
    up_out[...] = up
    wide = up.astype(F32)
    st[z] = pack_stats(
        jnp.sum(wide, axis=1, keepdims=True), jnp.sum(wide * wide, axis=1, keepdims=True)
    )
    sent = spread(st, ts, tr, "fsdp")
    collect(st, ts, tr, "fsdp", sent)
    total = st[0] + st[1] + st[2] + st[3]
    middle, inv = open_stats(total, width * 4)
    final = ((1.0 + mine[2:3]) * ((wide - middle) * inv) + mine[1:2]).astype(BF)
    vel[z] = lax.dot_general(
        hrows[...], final, (((1,), (1,)), ((), ())), preferred_element_type=F32
    )
    sent = spread(vel, vs, vr, "fsdp")
    collect(vel, vs, vr, "fsdp", sent)
    mix[pl.ds(0, 64), pl.ds(0, rows)] = vel[0] + vel[1] + vel[2] + vel[3]
    velocity = mix[pl.ds(0, 64), pl.ds(0, rows)]
    half = lats.shape[0]
    other = 1 - g
    swap[0] = mix[pl.ds(pl.multiple_of(other * half, half), half), pl.ds(0, rows)]
    cross = push(swap.at[0], swap.at[1], gs, gr, "guide", other)
    cross.start()
    full = jnp.sum(jnp.where(flags[0:1] > 0.0, total[1:2], 0.0), axis=1, keepdims=True)
    top = jnp.max(jnp.where(flags[1:2] > 0.0, velocity, -jnp.inf), axis=1, keepdims=True)
    top = jnp.max(top, axis=0, keepdims=True)
    line = lax.broadcasted_iota(jnp.int32, (8, 128), 0)
    tot[me] = jnp.where(line == 0, full, top)
    sent = spread(tot, ks, kr, "seq")
    collect(tot, ks, kr, "seq", sent)
    added = tot[0] + tot[1] + tot[2] + tot[3]
    peak = jnp.maximum(jnp.maximum(tot[0], tot[1]), jnp.maximum(tot[2], tot[3]))
    norm_out[...] = jnp.sqrt(added[0:1, 0:1] / consts[0:1, 2:3])
    peak_out[...] = peak[1:2, 0:1]
    cross.wait()
    own = mix[pl.ds(pl.multiple_of(g * half, half), half), pl.ds(0, rows)]
    theirs = swap[1]
    cond = jnp.where(g == 0, own, theirs)
    free = jnp.where(g == 0, theirs, own)
    guided = free + consts[0:1, 0:1] * (cond - free)
    lat_out[...] = jnp.where(flags[1:2] > 0.0, lats[...] + consts[0:1, 1:2] * guided, 0.0)
    for move in moves:
        move.wait_send()
    for d in range(4):
        @pl.when(z != d)
        def _():
            hop(d, 0).wait_send()


def back(q, k, v, act, kval, hid, keep, flags, mine, hrows, lats, consts, w):
    rows, width = hid.shape
    depth = w.shape[0]
    dma = pltpu.SemaphoreType.DMA
    shape = jax.ShapeDtypeStruct
    return pl.pallas_call(
        back_kernel,
        out_shape=(
            shape((rows, width), BF),
            shape(lats.shape, F32),
            shape((1, 1), F32),
            shape((1, 1), F32),
        ),
        in_specs=vmem(12) + [pl.BlockSpec(memory_space=pltpu.HBM)],
        out_specs=tuple(vmem(4)),
        scratch_shapes=[
            pltpu.VMEM((4,) + k.shape, BF),
            pltpu.VMEM((4,) + k.shape, BF),
            pltpu.VMEM((k.shape[1] // HD, rows, 1), F32),
            pltpu.VMEM((k.shape[1] // HD, rows, 1), F32),
            pltpu.VMEM(q.shape, F32),
            pltpu.VMEM(q.shape, BF),
            pltpu.VMEM((4, rows, width), F32),
            pltpu.VMEM((4, rows, width), BF),
            pltpu.VMEM((2, 4, rows, width), BF),
            pltpu.VMEM((4, depth, width), BF),
            pltpu.VMEM((4, 8, rows), F32),
            pltpu.VMEM((4, 64, rows), F32),
            pltpu.VMEM((rows, width), F32),
            pltpu.VMEM((2, lats.shape[0], rows), F32),
            pltpu.VMEM((4, 8, 128), F32),
            dma((6,)),
            dma((4,)),
            dma((4,)),
            dma((4,)),
            dma((2, 4)),
            dma((4,)),
            dma((3,)),
            dma((4,)),
            dma((3,)),
            dma((4,)),
            dma,
            dma,
            dma((3,)),
            dma((4,)),
        ],
        compiler_params=pltpu.CompilerParams(
            collective_id=2, has_side_effects=True, vmem_limit_bytes=60 << 20
        ),
        cost_estimate=pl.CostEstimate(
            flops=8 * rows * depth * width, bytes_accessed=8 * depth * width, transcendentals=0
        ),
    )(q, k, v, act, kval, hid, keep, flags, mine, hrows, lats, consts, w)


def fast_shards(
    hidden,
    modulation,
    in_weight,
    query_gain,
    key_gain,
    out_weight,
    head_weight,
    latents,
    step_size,
    guidance,
    text_len,
    tile_map,
):
    row_count, local_width = hidden.shape[1:]
    whole_out = lax.all_gather(out_weight, "guide", axis=1, tiled=True)
    first_row = lax.axis_index("seq") * row_count
    _, my_image, my_valid = describe(
        first_row + jnp.arange(row_count, dtype=jnp.int32), tile_map, text_len
    )
    keep = my_valid.astype(F32)[:, None]
    span = (in_weight.shape[1] - out_weight.shape[0]) // 2
    ss = modulation[0, 0, :2].reshape(2, 4, local_width).transpose(1, 0, 2)
    queries, keys, values, activated = front(
        hidden[0], keep, ss, query_gain[None], key_gain[None], in_weight, span
    )
    flags = jnp.concatenate(
        [my_valid.astype(F32)[None], my_image.astype(F32)[None], jnp.zeros((6, row_count), F32)]
    )
    start = lax.axis_index("fsdp") * local_width
    mine = lax.dynamic_slice_in_dim(modulation[0, 0, 2:], start, local_width, 1)
    head_rows = lax.dynamic_slice_in_dim(head_weight, start, local_width, 0).T
    channels = latents.shape[0] // 2
    my_latents = lax.dynamic_slice_in_dim(
        latents, lax.axis_index("guide") * channels, channels, 0
    )
    count = (IMG + text_len).astype(F32) * (local_width * 4)
    consts = jnp.concatenate([guidance, step_size, count, jnp.zeros((125,), F32)])[None]
    _, _, key_valid = describe(
        jnp.arange(row_count * 4, dtype=jnp.int32), tile_map, text_len
    )
    kval = key_valid.astype(F32).reshape(4, 1, row_count)
    updated, next_latents, norm, peak = back(
        queries, keys, values, activated, kval, hidden[0], keep, flags, mine, head_rows,
        my_latents, consts, whole_out,
    )
    return (updated[None], next_latents, norm, peak)


def solution(mesh):
    placed = (
        P("guide", "seq", "fsdp"),
        P("guide", None, None, None),
        P(None, "fsdp"),
        P(),
        P(),
        P("fsdp", "guide"),
        P(),
        P(None, "seq"),
        P(),
        P(),
        P(),
        P(),
    )
    shape = dict(mesh.shape)
    planned = shape["fsdp"] == 4 and shape["seq"] == 4 and shape["guide"] == 2
    return jax.shard_map(
        fast_shards if planned else shards,
        mesh=mesh,
        in_specs=placed,
        out_specs=(
            P("guide", "seq", "fsdp"),
            P("guide", "seq"),
            P("guide", None),
            P("guide", None),
        ),
        check_vma=False,
    )
```

```python
import jax
import jax.numpy as jnp
from jax import lax
from jax.experimental import pallas as pl
from jax.experimental.pallas import tpu as pltpu
from jax.sharding import PartitionSpec as P

HD = 128
TXT = 512
IMG = 1024
TILE = 128


def swapped(block, axis, stride):
    count = lax.axis_size(axis)
    route = []
    for low in range(count):
        high = low | 1 << stride
        if high != low and high < count:
            route += [(low, high), (high, low)]
    return lax.ppermute(block, axis, route)


def layer_norm(values):
    middle = jnp.mean(values, axis=-1, keepdims=True)
    power = jnp.mean(values * values, axis=-1, keepdims=True)
    return (values - middle) * lax.rsqrt(power - middle * middle + 1e-06)


def describe(index, tile_map, text_len):
    tile_index = index // TILE
    numbers = jnp.arange(tile_map.shape[0], dtype=jnp.int32)
    picked = jnp.sum(
        jnp.where(tile_index[:, None] == numbers[None, :], tile_map[None, :], 0), axis=1
    )
    logical = picked * TILE + index % TILE
    request = logical // (TXT + IMG)
    position = logical % (TXT + IMG)
    image = position >= TXT
    slots = jnp.arange(text_len.shape[0], dtype=jnp.int32)
    length = jnp.sum(jnp.where(request[:, None] == slots[None, :], text_len[None, :], 0), axis=1)
    valid = image | (position < length)
    return (request, image, valid)


def head_rms(values, gain):
    row_count = values.shape[0]
    shaped = values.reshape(row_count, -1, HD)
    scaled = shaped * lax.rsqrt(jnp.mean(shaped * shaped, axis=-1, keepdims=True) + 1e-06) * gain
    return scaled.reshape(row_count, -1).astype(jnp.bfloat16)


def shards(
    hidden,
    modulation,
    in_weight,
    query_gain,
    key_gain,
    out_weight,
    head_weight,
    latents,
    step_size,
    guidance,
    text_len,
    tile_map,
):
    row_count = hidden.shape[1]
    local_width = hidden.shape[2]
    requests = text_len.shape[0]
    first_row = lax.axis_index("seq") * row_count
    my_request, my_image, my_valid = describe(
        first_row + jnp.arange(row_count, dtype=jnp.int32), tile_map, text_len
    )
    request_hot = (my_request[:, None] == jnp.arange(requests, dtype=jnp.int32)[None, :]).astype(
        jnp.float32
    )

    def lookup(which):
        return jnp.dot(request_hot, modulation[0, :, which, :], precision=lax.Precision.HIGHEST)

    feature_start = lax.axis_index("fsdp") * local_width
    keep = my_valid[:, None]
    x_rows = hidden[0] * keep.astype(jnp.bfloat16)
    whole = lax.all_gather(x_rows, "fsdp", axis=1, tiled=True)
    normed = layer_norm(whole.astype(jnp.float32))
    modded = ((1.0 + lookup(1)) * normed + lookup(0)).astype(jnp.bfloat16)
    col_width = in_weight.shape[1]
    projected = jnp.dot(modded, in_weight, preferred_element_type=jnp.float32)
    span = (col_width - out_weight.shape[0]) // 2
    head_count = span // HD
    queries = head_rms(projected[:, :span], query_gain)
    keys = head_rms(projected[:, span : 2 * span], key_gain)
    values = projected[:, 2 * span : 3 * span].astype(jnp.bfloat16)
    mlp_part = projected[:, 3 * span :]
    query_heads = queries.reshape(row_count, head_count, HD)
    factor = HD ** (-0.5)
    key_piece = lax.all_gather(keys, "seq", axis=0, tiled=True)
    value_piece = lax.all_gather(values, "seq", axis=0, tiled=True)
    width = key_piece.shape[0]
    key_request, key_image, key_valid = describe(
        jnp.arange(width, dtype=jnp.int32), tile_map, text_len
    )
    allowed = (my_request[:, None] == key_request[None, :]) & key_valid[None, :]
    run_max = jnp.full((head_count, row_count), -1e30, jnp.float32)
    key_heads = key_piece.reshape(width, head_count, HD)
    value_heads = value_piece.reshape(width, head_count, HD)
    scores = (
        jnp.einsum("qhd,khd->hqk", query_heads, key_heads, preferred_element_type=jnp.float32)
        * factor
    )
    scores = jnp.where(allowed[None, :, :], scores, -jnp.inf)
    new_max = jnp.maximum(run_max, jnp.max(scores, axis=-1))
    raised = jnp.exp(scores - new_max[:, :, None])
    new_total = jnp.sum(raised, axis=-1)
    added = jnp.einsum(
        "hqk,khd->hqd", raised.astype(jnp.bfloat16), value_heads, preferred_element_type=jnp.float32
    )
    attended = (
        (added / new_total[:, :, None])
        .transpose(1, 0, 2)
        .reshape(row_count, span)
        .astype(jnp.bfloat16)
    )
    activated = jax.nn.gelu(mlp_part, approximate=True).astype(jnp.bfloat16)
    branch = jnp.concatenate([attended, activated], axis=1)
    terms = jnp.dot(
        branch,
        lax.all_gather(out_weight, "guide", axis=1, tiled=True),
        preferred_element_type=jnp.float32,
    )
    mixed = lax.psum_scatter(terms, "fsdp", scatter_dimension=1, tiled=True)
    gate = lax.dynamic_slice_in_dim(lookup(2), feature_start, local_width, 1)
    updated = ((x_rows.astype(jnp.float32) + gate * mixed) * keep.astype(jnp.float32)).astype(
        jnp.bfloat16
    )
    up_values = updated.astype(jnp.float32)
    contract = (((0,), (1,)), ((), ()))
    full_width = local_width * lax.axis_size("fsdp")
    row_sums, row_squares = lax.psum(
        (jnp.sum(up_values, axis=1), jnp.sum(up_values * up_values, axis=1)), "fsdp"
    )
    middle = (row_sums / full_width)[:, None]
    power = (row_squares / full_width)[:, None]
    local_normed = (up_values - middle) * lax.rsqrt(power - middle * middle + 1e-06)
    head_scale = lax.dynamic_slice_in_dim(lookup(4), feature_start, local_width, 1)
    head_shift = lax.dynamic_slice_in_dim(lookup(3), feature_start, local_width, 1)
    final = ((1.0 + head_scale) * local_normed + head_shift).astype(jnp.bfloat16)
    head_rows = lax.dynamic_slice_in_dim(head_weight, feature_start, local_width, 0)
    head_part = lax.dot_general(head_rows, final, contract, preferred_element_type=jnp.float32)
    velocity = lax.psum(head_part, "fsdp")
    partner = swapped(velocity.astype(jnp.bfloat16), "guide", 0).astype(velocity.dtype)
    is_first = lax.axis_index("guide") == 0
    cond_velocity = jnp.where(is_first, velocity, partner)
    uncond_velocity = jnp.where(is_first, partner, velocity)
    guide_rows = jnp.dot(request_hot, guidance, precision=lax.Precision.HIGHEST)
    step_rows = jnp.dot(request_hot, step_size, precision=lax.Precision.HIGHEST)
    guided = uncond_velocity + guide_rows[None, :] * (cond_velocity - uncond_velocity)
    channel_count = latents.shape[0] // lax.axis_size("guide")
    channel_start = lax.axis_index("guide") * channel_count
    my_guided = lax.dynamic_slice_in_dim(guided, channel_start, channel_count, 0)
    my_latents = lax.dynamic_slice_in_dim(latents, channel_start, channel_count, 0)
    next_latents = jnp.where(my_image[None, :], my_latents + step_rows[None, :] * my_guided, 0.0)
    member = my_request[None, :] == jnp.arange(requests, dtype=jnp.int32)[:, None]
    squares = jnp.sum(up_values * up_values, axis=1)
    local_total = jnp.sum(jnp.where(member & my_valid[None, :], squares[None, :], 0.0), axis=1)
    picked = jnp.where((member & my_image[None, :])[:, None, :], velocity[None, :, :], -jnp.inf)
    local_peak = jnp.max(picked, axis=(1, 2))
    total = lax.psum(local_total, ("seq", "fsdp"))
    peak = lax.pmax(local_peak, "seq")
    count = (IMG + text_len).astype(jnp.float32) * (local_width * lax.axis_size("fsdp"))
    hidden_norm = jnp.sqrt(total / count)
    return (updated[None], next_latents, hidden_norm[None], peak[None])


MESH = pl.DeviceIdType.MESH
BF = jnp.bfloat16
F32 = jnp.float32


def greet(axes):
    barrier = pltpu.get_barrier_semaphore()
    count = 0
    for axis in axes:
        size = lax.axis_size(axis)
        me = lax.axis_index(axis)
        for step in range(1, size):
            pl.semaphore_signal(
                barrier, inc=1, device_id={axis: lax.rem(me + step, size)}, device_id_type=MESH
            )
        count += size - 1
    pl.semaphore_wait(barrier, count)


def push(src, dst, send, recv, axis, target):
    return pltpu.make_async_remote_copy(
        src_ref=src,
        dst_ref=dst,
        send_sem=send,
        recv_sem=recv,
        device_id={axis: target},
        device_id_type=MESH,
    )


def spread(buf, send, recv, axis):
    size = lax.axis_size(axis)
    me = lax.axis_index(axis)
    copies = [
        push(buf.at[me], buf.at[me], send.at[s - 1], recv.at[me], axis, lax.rem(me + s, size))
        for s in range(1, size)
    ]
    for copy in copies:
        copy.start()
    return copies


def collect(buf, send, recv, axis, copies):
    size = lax.axis_size(axis)
    me = lax.axis_index(axis)
    for copy in copies:
        copy.wait_send()
    for s in range(1, size):
        other = lax.rem(me + s, size)
        push(buf.at[other], buf.at[other], send.at[s - 1], recv.at[other], axis, other).wait_recv()


def pack_stats(sums, squares):
    rows = sums.shape[0]
    lane = lax.broadcasted_iota(jnp.int32, (rows, 128), 1)
    both = jnp.where(lane == 0, sums, jnp.where(lane == 1, squares, 0.0))
    return jnp.transpose(both)[:8]


def open_stats(total, width):
    rows = total.shape[1]
    tall = jnp.concatenate([total, jnp.zeros((120, rows), F32)], axis=0)
    back = jnp.transpose(tall)
    middle = back[:, 0:1] / width
    power = back[:, 1:2] / width
    return middle, lax.rsqrt(power - middle * middle + 1e-06)


def places(tmap, tlen, first, shape, dim):
    spot = lax.broadcasted_iota(jnp.int32, shape, dim)
    base = jnp.zeros(shape, jnp.int32)
    for j in range(shape[dim] // TILE):
        base = jnp.where(spot >= j * TILE, (tmap[first + j] - j) * TILE, base)
    where = spot + base
    image = where >= TXT
    return image, image | (where < tlen[0])


def row_keep(tmap, tlen, me, rows):
    _, valid = places(tmap, tlen, me * (rows // TILE), (rows, 1), 0)
    return jnp.where(valid, 1.0, 0.0)


def pick(z, values):
    out = values[-1]
    for i in range(len(values) - 2, -1, -1):
        out = jnp.where(z == i, values[i], out)
    return out


def front_kernel(
    tmap, tlen, hid, ss, qg, kg, w, q_out, k_out, v_out, act_out,
    xg, st, acc, wbuf, mod, xs, xr, ts, tr, ws,
):
    z = lax.axis_index("fsdp")
    rows, part = hid.shape
    width = part * 4
    span = q_out.shape[1]
    tiles = acc.shape[1] // span
    keep = row_keep(tmap, tlen, lax.axis_index("seq"), rows)
    order = [
        z,
        pick(z, [1, 0, 3, 2]),
        pick(z, [2, 2, 1, 1]),
        pick(z, [3, 3, 0, 0]),
    ]

    def wcopy(p):
        at = pl.multiple_of(order[p] * part, part)
        return pltpu.make_async_copy(w.at[pl.ds(at, part), :], wbuf.at[p], ws.at[p])

    for p in range(4):
        wcopy(p).start()
    greet(("fsdp",))
    xg[z] = hid[...]

    def hop(c, way):
        target = jnp.minimum(z + 1, 3) if way == 0 else jnp.maximum(z - 1, 0)
        return push(xg.at[c], xg.at[c], xs.at[way, c], xr.at[c], "fsdp", target)

    @pl.when(z < 3)
    def _():
        hop(z, 0).start()

    @pl.when(z > 0)
    def _():
        hop(z, 1).start()

    own = (hid[...].astype(F32)) * keep
    st[z] = pack_stats(
        jnp.sum(own, axis=1, keepdims=True), jnp.sum(own * own, axis=1, keepdims=True)
    )
    sent = spread(st, ts, tr, "fsdp")
    collect(st, ts, tr, "fsdp", sent)
    middle, inv = open_stats(st[0] + st[1] + st[2] + st[3], width)

    def arrive(c):
        hop(c, 0).wait_recv()

        @pl.when((c < z) & (z < 3))
        def _():
            hop(c, 0).start()

        @pl.when((c > z) & (z > 0))
        def _():
            hop(c, 1).start()

    inner = (z > 0) & (z < 3)
    for p in range(4):
        c = order[p]
        if p == 1:
            arrive(c)

            @pl.when(inner)
            def _():
                arrive(order[2])
        if p == 2:
            @pl.when(jnp.logical_not(inner))
            def _():
                arrive(order[2])
        if p == 3:
            arrive(c)
        vals = xg[c].astype(F32) * keep
        cut = pl.ds(pl.multiple_of(c * part, part), part)
        mod[...] = ((1.0 + ss[1:2, cut]) * ((vals - middle) * inv) + ss[0:1, cut]).astype(BF)
        wcopy(p).wait()

        def value(i):
            at = pl.ds(pl.multiple_of(i * span, span), span)
            return at, jnp.dot(mod[...], wbuf[p, :, at], preferred_element_type=F32)

        def tile(i, carry):
            at, got = value(i)
            if p == 0:
                acc[:, at] = got
            else:
                acc[:, at] += got
            return carry

        def last(i, carry):
            at, got = value(i)
            to = pl.ds(pl.multiple_of((i - 3) * span, span), span)
            act_out[:, to] = jax.nn.gelu(acc[:, at] + got, approximate=True).astype(BF)
            return carry

        if p < 3:
            lax.fori_loop(0, tiles, tile, 0)
        else:
            for i, gain, dst in ((1, kg, k_out), (2, None, v_out), (0, qg, q_out)):
                at, got = value(i)
                got = acc[:, at] + got
                if gain is None:
                    dst[...] = got.astype(BF)
                    continue
                for h in range(span // HD):
                    cols = slice(h * HD, (h + 1) * HD)
                    vals = got[:, cols]
                    scaled = vals * lax.rsqrt(
                        jnp.mean(vals * vals, axis=1, keepdims=True) + 1e-06
                    )
                    dst[:, cols] = (scaled * gain[...]).astype(BF)
            lax.fori_loop(3, tiles, last, 0)

    for c in range(4):
        @pl.when((z < 3) & (z >= c))
        def _():
            hop(c, 0).wait_send()

        @pl.when((z > 0) & (z <= c))
        def _():
            hop(c, 1).wait_send()


def vmem(count):
    return [pl.BlockSpec(memory_space=pltpu.VMEM)] * count


def smem(count):
    return [pl.BlockSpec(memory_space=pltpu.SMEM)] * count


def front(tmap, tlen, hid, ss, qg, kg, w, span):
    rows, part = hid.shape
    cols = w.shape[1]
    dma = pltpu.SemaphoreType.DMA
    shape = jax.ShapeDtypeStruct
    return pl.pallas_call(
        front_kernel,
        out_shape=(
            shape((rows, span), BF),
            shape((rows, span), BF),
            shape((rows, span), BF),
            shape((rows, cols - 3 * span), BF),
        ),
        in_specs=smem(2) + vmem(4) + [pl.BlockSpec(memory_space=pltpu.HBM)],
        out_specs=tuple(vmem(4)),
        scratch_shapes=[
            pltpu.VMEM((4, rows, part), BF),
            pltpu.VMEM((4, 8, rows), F32),
            pltpu.VMEM((rows, cols), F32),
            pltpu.VMEM((4, part, cols), BF),
            pltpu.VMEM((rows, part), BF),
            dma((2, 4)),
            dma((4,)),
            dma((3,)),
            dma((4,)),
            dma((4,)),
        ],
        compiler_params=pltpu.CompilerParams(
            collective_id=1, has_side_effects=True, vmem_limit_bytes=60 << 20
        ),
        cost_estimate=pl.CostEstimate(
            flops=2 * rows * 4 * part * cols, bytes_accessed=8 * part * cols, transcendentals=0
        ),
    )(tmap, tlen, hid, ss, qg, kg, w)


def back_kernel(
    tmap, tlen, guide, step, q, k, v, act, hid, md, head, lats, w,
    up_out, lat_out, norm_out, peak_out,
    kbuf, vbuf, high, low, gain, att, part, sbuf, rbuf, wbuf, st, vel, vsend, vrec, line, mix, swap, tot,
    ps, kq, vq, ss, rs, ws, ts, tr, us, ur, vs, vr, gs, gr, ks, kr,
):
    z = lax.axis_index("fsdp")
    g = lax.axis_index("guide")
    me = lax.axis_index("seq")
    rows, width = hid.shape
    tiles = rows // TILE
    cut = pl.ds(pl.multiple_of(z * width, width), width)
    keep = row_keep(tmap, tlen, me, rows)
    my_image, my_valid = places(tmap, tlen, me * tiles, (1, rows), 1)
    order = [
        pick(z, [3, 3, 0, 0]),
        pick(z, [2, 0, 3, 1]),
        pick(z, [1, 2, 1, 2]),
        z,
    ]

    def wcopy(p):
        at = pl.multiple_of(order[p] * width, width)
        return pltpu.make_async_copy(w.at[:, pl.ds(at, width)], wbuf.at[p], ws.at[p])

    for p in range(4):
        wcopy(p).start()
    kbuf[me] = k[...]
    vbuf[me] = v[...]
    greet(("fsdp", "seq", "guide"))
    near_x = me + 1 - 2 * lax.rem(me, 2)
    near_y = lax.rem(me + 2, 4)
    across = 3 - me

    def key_hop(src, at, target):
        return push(kbuf.at[src], kbuf.at[src], ps.at[at], kq.at[src], "seq", target)

    def value_hop(src, at, target):
        return push(vbuf.at[src], vbuf.at[src], ps.at[at], vq.at[src], "seq", target)

    moves = [
        key_hop(me, 0, near_x),
        value_hop(me, 1, near_y),
        key_hop(me, 2, near_y),
        value_hop(me, 3, near_x),
        key_hop(near_x, 4, near_y),
        value_hop(near_y, 5, near_x),
    ]
    for move in moves[:4]:
        move.start()

    span = q.shape[1]
    rate = HD ** (-0.5) * 1.4426950408889634

    def attend(src, first):
        _, open_keys = places(tmap, tlen, src * tiles, (1, rows), 1)

        def heads(i, carry):
            for j in range(2):
                h = i * 2 + j
                at = pl.ds(pl.multiple_of(h * HD, HD), HD)
                s = lax.dot_general(
                    q[:, at],
                    kbuf[src, :, at],
                    (((1,), (1,)), ((), ())),
                    preferred_element_type=F32,
                )
                s = jnp.where(open_keys, s, -1e30)
                top = jnp.max(s, axis=1, keepdims=True)
                if not first:
                    top = jnp.maximum(top, high[h])
                p = jnp.exp2((s - top) * rate)
                total = jnp.sum(p, axis=1, keepdims=True)
                got = jnp.dot(p.astype(BF), vbuf[src, :, at], preferred_element_type=F32)
                if not first:
                    shrink = jnp.exp2((high[h] - top) * rate)
                    total = total + low[h] * shrink
                    got = got + gain[:, at] * shrink
                high[h] = top
                low[h] = total
                gain[:, at] = got
            return carry

        lax.fori_loop(0, span // (2 * HD), heads, 0)

    def hop(d, way):
        target = jnp.minimum(z + 1, 3) if way == 0 else jnp.maximum(z - 1, 0)
        return push(sbuf.at[d], rbuf.at[way, d], ss.at[d], rs.at[way, d], "fsdp", target)

    ends = (z == 0) | (z == 3)
    attend(me, True)
    for p in range(4):
        d = order[p]
        wcopy(p).wait()

        def tile(i, carry):
            at = pl.ds(pl.multiple_of(i * 256, 256), 256)
            part[d, :, at] = jnp.dot(act[...], wbuf[p, span:, at], preferred_element_type=F32)
            return carry

        lax.fori_loop(0, width // 256, tile, 0)
        if p == 2:
            key_hop(near_x, 0, near_x).wait_recv()
            moves[4].start()
            value_hop(near_y, 1, near_y).wait_recv()
            moves[5].start()
    value_hop(near_x, 3, near_x).wait_recv()
    attend(near_x, False)
    key_hop(near_y, 2, near_y).wait_recv()
    attend(near_y, False)
    key_hop(across, 4, near_y).wait_recv()
    value_hop(across, 5, near_x).wait_recv()
    attend(across, False)
    for h in range(span // HD):
        at = slice(h * HD, (h + 1) * HD)
        att[:, at] = (gain[:, at] / low[h]).astype(BF)
    for p in range(4):
        d = order[p]

        def tile(i, carry):
            at = pl.ds(pl.multiple_of(i * 256, 256), 256)
            part[d, :, at] += jnp.dot(att[...], wbuf[p, :span, at], preferred_element_type=F32)
            return carry

        lax.fori_loop(0, width // 256, tile, 0)
        if p < 3:
            @pl.when(z == 0)
            def _():
                sbuf[d] = part[d].astype(BF)
                hop(d, 0).start()

            @pl.when(z == 3)
            def _():
                sbuf[d] = part[d].astype(BF)
                hop(d, 1).start()

    def relay(d, way):
        hop(d, way).wait_recv()
        sbuf[d] = (part[d] + rbuf[way, d].astype(F32)).astype(BF)
        hop(d, way).start()

    @pl.when(z == 1)
    def _():
        relay(3, 0)
        relay(2, 0)
        relay(0, 1)

    @pl.when(z == 2)
    def _():
        relay(0, 1)
        relay(1, 1)
        relay(3, 0)

    mix[...] = part[z]

    @pl.when(z > 0)
    def _():
        hop(z, 0).wait_recv()
        mix[...] += rbuf[0, z].astype(F32)

    @pl.when(z < 3)
    def _():
        hop(z, 1).wait_recv()
        mix[...] += rbuf[1, z].astype(F32)

    x = hid[...].astype(F32) * keep
    up = ((x + md[2:3, cut] * mix[...]) * keep).astype(BF)
    up_out[...] = up
    wide = up.astype(F32)
    st[z] = pack_stats(
        jnp.sum(wide, axis=1, keepdims=True), jnp.sum(wide * wide, axis=1, keepdims=True)
    )
    stats_sent = spread(st, ts, tr, "fsdp")
    vpart = lax.dot_general(
        head[:, cut].astype(F32),
        wide * (1.0 + md[4:5, cut]),
        (((1,), (1,)), ((), ())),
        precision=lax.Precision.HIGHEST,
        preferred_element_type=F32,
    )
    share = vsend.shape[1]
    for d in range(4):
        vsend[d] = vpart[d * share : (d + 1) * share]

    def give(d, source, at):
        return push(vsend.at[d], vrec.at[source], us.at[at], ur.at[source], "fsdp", d)

    for s in range(1, 4):
        give(lax.rem(z + s, 4), z, s - 1).start()
    my_head = head[pl.ds(pl.multiple_of(z * share, share), share), :].astype(F32)
    scale_sum = jnp.sum(my_head * (1.0 + md[4:5, :]), axis=1, keepdims=True)
    shift_sum = jnp.sum(my_head * md[3:4, :], axis=1, keepdims=True)
    collect(st, ts, tr, "fsdp", stats_sent)
    total = st[0] + st[1] + st[2] + st[3]
    middle = total[0:1] / (width * 4)
    power = total[1:2] / (width * 4)
    inv = lax.rsqrt(power - middle * middle + 1e-06)
    mine = vsend[z]
    for s in range(1, 4):
        other = lax.rem(z + s, 4)
        give(other, other, s - 1).wait_recv()
        mine = mine + vrec[other]
    vel[z] = inv * (mine - middle * scale_sum) + shift_sum
    sent = spread(vel, vs, vr, "fsdp")
    collect(vel, vs, vr, "fsdp", sent)
    for d in range(4):
        line[d * share : (d + 1) * share, :] = vel[d]
    velocity = line[...]
    half = lats.shape[0] // 2
    other = 1 - g
    swap[0] = line[pl.ds(pl.multiple_of(other * half, half), half), :]
    cross = push(swap.at[0], swap.at[1], gs, gr, "guide", other)
    cross.start()
    full = jnp.sum(jnp.where(my_valid, total[1:2], 0.0), axis=1, keepdims=True)
    top = jnp.max(jnp.where(my_image, velocity, -jnp.inf), axis=1, keepdims=True)
    top = jnp.max(top, axis=0, keepdims=True)
    level = lax.broadcasted_iota(jnp.int32, (8, 128), 0)
    tot[me] = jnp.where(level == 0, full, top)
    sent = spread(tot, ks, kr, "seq")
    collect(tot, ks, kr, "seq", sent)
    added = tot[0] + tot[1] + tot[2] + tot[3]
    peak = jnp.maximum(jnp.maximum(tot[0], tot[1]), jnp.maximum(tot[2], tot[3]))
    count = (IMG + tlen[0]).astype(F32) * (width * 4)
    norm_out[...] = jnp.sqrt(added[0:1, 0:1] / count)
    peak_out[...] = peak[1:2, 0:1]
    cross.wait()
    own = line[pl.ds(pl.multiple_of(g * half, half), half), :]
    theirs = swap[1]
    cond = jnp.where(g == 0, own, theirs)
    free = jnp.where(g == 0, theirs, own)
    guided = free + guide[0] * (cond - free)
    mine = lats[pl.ds(pl.multiple_of(g * half, half), half), :]
    lat_out[...] = jnp.where(my_image, mine + step[0] * guided, 0.0)
    for move in moves:
        move.wait_send()
    for s in range(1, 4):
        give(lax.rem(z + s, 4), z, s - 1).wait_send()
    for d in range(4):
        @pl.when(z != d)
        def _():
            hop(d, 0).wait_send()


def back(tmap, tlen, guide, step, q, k, v, act, hid, md, head, lats, w):
    rows, width = hid.shape
    depth = w.shape[0]
    dma = pltpu.SemaphoreType.DMA
    shape = jax.ShapeDtypeStruct
    return pl.pallas_call(
        back_kernel,
        out_shape=(
            shape((rows, width), BF),
            shape((lats.shape[0] // 2, rows), F32),
            shape((1, 1), F32),
            shape((1, 1), F32),
        ),
        in_specs=smem(4) + vmem(8) + [pl.BlockSpec(memory_space=pltpu.HBM)],
        out_specs=tuple(vmem(4)),
        scratch_shapes=[
            pltpu.VMEM((4,) + k.shape, BF),
            pltpu.VMEM((4,) + k.shape, BF),
            pltpu.VMEM((k.shape[1] // HD, rows, 1), F32),
            pltpu.VMEM((k.shape[1] // HD, rows, 1), F32),
            pltpu.VMEM(q.shape, F32),
            pltpu.VMEM(q.shape, BF),
            pltpu.VMEM((4, rows, width), F32),
            pltpu.VMEM((4, rows, width), BF),
            pltpu.VMEM((2, 4, rows, width), BF),
            pltpu.VMEM((4, depth, width), BF),
            pltpu.VMEM((4, 8, rows), F32),
            pltpu.VMEM((4, lats.shape[0] // 4, rows), F32),
            pltpu.VMEM((4, lats.shape[0] // 4, rows), F32),
            pltpu.VMEM((4, lats.shape[0] // 4, rows), F32),
            pltpu.VMEM(lats.shape, F32),
            pltpu.VMEM((rows, width), F32),
            pltpu.VMEM((2, lats.shape[0] // 2, rows), F32),
            pltpu.VMEM((4, 8, 128), F32),
            dma((6,)),
            dma((4,)),
            dma((4,)),
            dma((4,)),
            dma((2, 4)),
            dma((4,)),
            dma((3,)),
            dma((4,)),
            dma((3,)),
            dma((4,)),
            dma((3,)),
            dma((4,)),
            dma,
            dma,
            dma((3,)),
            dma((4,)),
        ],
        compiler_params=pltpu.CompilerParams(
            collective_id=2, has_side_effects=True, vmem_limit_bytes=60 << 20
        ),
        cost_estimate=pl.CostEstimate(
            flops=8 * rows * depth * width, bytes_accessed=8 * depth * width, transcendentals=0
        ),
    )(tmap, tlen, guide, step, q, k, v, act, hid, md, head, lats, w)


def fast_shards(
    hidden,
    modulation,
    in_weight,
    query_gain,
    key_gain,
    out_weight,
    head_weight,
    latents,
    step_size,
    guidance,
    text_len,
    tile_map,
):
    whole_out = lax.all_gather(out_weight, "guide", axis=1, tiled=True)
    span = (in_weight.shape[1] - out_weight.shape[0]) // 2
    rows5 = modulation[0, 0]
    queries, keys, values, activated = front(
        tile_map, text_len, hidden[0], rows5, query_gain[None], key_gain[None], in_weight, span
    )
    updated, next_latents, norm, peak = back(
        tile_map, text_len, guidance, step_size, queries, keys, values, activated, hidden[0],
        rows5, head_weight.T, latents, whole_out,
    )
    return (updated[None], next_latents, norm, peak)


def solution(mesh):
    placed = (
        P("guide", "seq", "fsdp"),
        P("guide", None, None, None),
        P(None, "fsdp"),
        P(),
        P(),
        P("fsdp", "guide"),
        P(),
        P(None, "seq"),
        P(),
        P(),
        P(),
        P(),
    )
    shape = dict(mesh.shape)
    planned = shape["fsdp"] == 4 and shape["seq"] == 4 and shape["guide"] == 2

    def chosen(*args):
        return (fast_shards if planned and args[10].shape[0] == 1 else shards)(*args)

    return jax.shard_map(
        chosen,
        mesh=mesh,
        in_specs=placed,
        out_specs=(
            P("guide", "seq", "fsdp"),
            P("guide", "seq"),
            P("guide", None),
            P("guide", None),
        ),
        check_vma=False,
    )
```

```python
import jax
import jax.numpy as jnp
from jax import lax
from jax.experimental import pallas as pl
from jax.experimental.pallas import tpu as pltpu
from jax.sharding import PartitionSpec as P

HD = 128
TXT = 512
IMG = 1024
TILE = 128


def swapped(block, axis, stride):
    count = lax.axis_size(axis)
    route = []
    for low in range(count):
        high = low | 1 << stride
        if high != low and high < count:
            route += [(low, high), (high, low)]
    return lax.ppermute(block, axis, route)


def layer_norm(values):
    middle = jnp.mean(values, axis=-1, keepdims=True)
    power = jnp.mean(values * values, axis=-1, keepdims=True)
    return (values - middle) * lax.rsqrt(power - middle * middle + 1e-06)


def describe(index, tile_map, text_len):
    tile_index = index // TILE
    numbers = jnp.arange(tile_map.shape[0], dtype=jnp.int32)
    picked = jnp.sum(
        jnp.where(tile_index[:, None] == numbers[None, :], tile_map[None, :], 0), axis=1
    )
    logical = picked * TILE + index % TILE
    request = logical // (TXT + IMG)
    position = logical % (TXT + IMG)
    image = position >= TXT
    slots = jnp.arange(text_len.shape[0], dtype=jnp.int32)
    length = jnp.sum(jnp.where(request[:, None] == slots[None, :], text_len[None, :], 0), axis=1)
    valid = image | (position < length)
    return (request, image, valid)


def head_rms(values, gain):
    row_count = values.shape[0]
    shaped = values.reshape(row_count, -1, HD)
    scaled = shaped * lax.rsqrt(jnp.mean(shaped * shaped, axis=-1, keepdims=True) + 1e-06) * gain
    return scaled.reshape(row_count, -1).astype(jnp.bfloat16)


def shards(
    hidden,
    modulation,
    in_weight,
    query_gain,
    key_gain,
    out_weight,
    head_weight,
    latents,
    step_size,
    guidance,
    text_len,
    tile_map,
):
    row_count = hidden.shape[1]
    local_width = hidden.shape[2]
    requests = text_len.shape[0]
    first_row = lax.axis_index("seq") * row_count
    my_request, my_image, my_valid = describe(
        first_row + jnp.arange(row_count, dtype=jnp.int32), tile_map, text_len
    )
    request_hot = (my_request[:, None] == jnp.arange(requests, dtype=jnp.int32)[None, :]).astype(
        jnp.float32
    )

    def lookup(which):
        return jnp.dot(request_hot, modulation[0, :, which, :], precision=lax.Precision.HIGHEST)

    feature_start = lax.axis_index("fsdp") * local_width
    keep = my_valid[:, None]
    x_rows = hidden[0] * keep.astype(jnp.bfloat16)
    whole = lax.all_gather(x_rows, "fsdp", axis=1, tiled=True)
    normed = layer_norm(whole.astype(jnp.float32))
    modded = ((1.0 + lookup(1)) * normed + lookup(0)).astype(jnp.bfloat16)
    col_width = in_weight.shape[1]
    projected = jnp.dot(modded, in_weight, preferred_element_type=jnp.float32)
    span = (col_width - out_weight.shape[0]) // 2
    head_count = span // HD
    queries = head_rms(projected[:, :span], query_gain)
    keys = head_rms(projected[:, span : 2 * span], key_gain)
    values = projected[:, 2 * span : 3 * span].astype(jnp.bfloat16)
    mlp_part = projected[:, 3 * span :]
    query_heads = queries.reshape(row_count, head_count, HD)
    factor = HD ** (-0.5)
    key_piece = lax.all_gather(keys, "seq", axis=0, tiled=True)
    value_piece = lax.all_gather(values, "seq", axis=0, tiled=True)
    width = key_piece.shape[0]
    key_request, key_image, key_valid = describe(
        jnp.arange(width, dtype=jnp.int32), tile_map, text_len
    )
    allowed = (my_request[:, None] == key_request[None, :]) & key_valid[None, :]
    run_max = jnp.full((head_count, row_count), -1e30, jnp.float32)
    key_heads = key_piece.reshape(width, head_count, HD)
    value_heads = value_piece.reshape(width, head_count, HD)
    scores = (
        jnp.einsum("qhd,khd->hqk", query_heads, key_heads, preferred_element_type=jnp.float32)
        * factor
    )
    scores = jnp.where(allowed[None, :, :], scores, -jnp.inf)
    new_max = jnp.maximum(run_max, jnp.max(scores, axis=-1))
    raised = jnp.exp(scores - new_max[:, :, None])
    new_total = jnp.sum(raised, axis=-1)
    added = jnp.einsum(
        "hqk,khd->hqd", raised.astype(jnp.bfloat16), value_heads, preferred_element_type=jnp.float32
    )
    attended = (
        (added / new_total[:, :, None])
        .transpose(1, 0, 2)
        .reshape(row_count, span)
        .astype(jnp.bfloat16)
    )
    activated = jax.nn.gelu(mlp_part, approximate=True).astype(jnp.bfloat16)
    branch = jnp.concatenate([attended, activated], axis=1)
    terms = jnp.dot(
        branch,
        lax.all_gather(out_weight, "guide", axis=1, tiled=True),
        preferred_element_type=jnp.float32,
    )
    mixed = lax.psum_scatter(terms, "fsdp", scatter_dimension=1, tiled=True)
    gate = lax.dynamic_slice_in_dim(lookup(2), feature_start, local_width, 1)
    updated = ((x_rows.astype(jnp.float32) + gate * mixed) * keep.astype(jnp.float32)).astype(
        jnp.bfloat16
    )
    up_values = updated.astype(jnp.float32)
    contract = (((0,), (1,)), ((), ()))
    full_width = local_width * lax.axis_size("fsdp")
    row_sums, row_squares = lax.psum(
        (jnp.sum(up_values, axis=1), jnp.sum(up_values * up_values, axis=1)), "fsdp"
    )
    middle = (row_sums / full_width)[:, None]
    power = (row_squares / full_width)[:, None]
    local_normed = (up_values - middle) * lax.rsqrt(power - middle * middle + 1e-06)
    head_scale = lax.dynamic_slice_in_dim(lookup(4), feature_start, local_width, 1)
    head_shift = lax.dynamic_slice_in_dim(lookup(3), feature_start, local_width, 1)
    final = ((1.0 + head_scale) * local_normed + head_shift).astype(jnp.bfloat16)
    head_rows = lax.dynamic_slice_in_dim(head_weight, feature_start, local_width, 0)
    head_part = lax.dot_general(head_rows, final, contract, preferred_element_type=jnp.float32)
    velocity = lax.psum(head_part, "fsdp")
    partner = swapped(velocity.astype(jnp.bfloat16), "guide", 0).astype(velocity.dtype)
    is_first = lax.axis_index("guide") == 0
    cond_velocity = jnp.where(is_first, velocity, partner)
    uncond_velocity = jnp.where(is_first, partner, velocity)
    guide_rows = jnp.dot(request_hot, guidance, precision=lax.Precision.HIGHEST)
    step_rows = jnp.dot(request_hot, step_size, precision=lax.Precision.HIGHEST)
    guided = uncond_velocity + guide_rows[None, :] * (cond_velocity - uncond_velocity)
    channel_count = latents.shape[0] // lax.axis_size("guide")
    channel_start = lax.axis_index("guide") * channel_count
    my_guided = lax.dynamic_slice_in_dim(guided, channel_start, channel_count, 0)
    my_latents = lax.dynamic_slice_in_dim(latents, channel_start, channel_count, 0)
    next_latents = jnp.where(my_image[None, :], my_latents + step_rows[None, :] * my_guided, 0.0)
    member = my_request[None, :] == jnp.arange(requests, dtype=jnp.int32)[:, None]
    squares = jnp.sum(up_values * up_values, axis=1)
    local_total = jnp.sum(jnp.where(member & my_valid[None, :], squares[None, :], 0.0), axis=1)
    picked = jnp.where((member & my_image[None, :])[:, None, :], velocity[None, :, :], -jnp.inf)
    local_peak = jnp.max(picked, axis=(1, 2))
    total = lax.psum(local_total, ("seq", "fsdp"))
    peak = lax.pmax(local_peak, "seq")
    count = (IMG + text_len).astype(jnp.float32) * (local_width * lax.axis_size("fsdp"))
    hidden_norm = jnp.sqrt(total / count)
    return (updated[None], next_latents, hidden_norm[None], peak[None])


MESH = pl.DeviceIdType.MESH
BF = jnp.bfloat16
F32 = jnp.float32


def greet(axes):
    barrier = pltpu.get_barrier_semaphore()
    count = 0
    for axis in axes:
        size = lax.axis_size(axis)
        me = lax.axis_index(axis)
        for step in range(1, size):
            pl.semaphore_signal(
                barrier, inc=1, device_id={axis: lax.rem(me + step, size)}, device_id_type=MESH
            )
        count += size - 1
    pl.semaphore_wait(barrier, count)


def push(src, dst, send, recv, axis, target):
    return pltpu.make_async_remote_copy(
        src_ref=src,
        dst_ref=dst,
        send_sem=send,
        recv_sem=recv,
        device_id={axis: target},
        device_id_type=MESH,
    )


def spread(buf, send, recv, axis):
    size = lax.axis_size(axis)
    me = lax.axis_index(axis)
    copies = [
        push(buf.at[me], buf.at[me], send.at[s - 1], recv.at[me], axis, lax.rem(me + s, size))
        for s in range(1, size)
    ]
    for copy in copies:
        copy.start()
    return copies


def collect(buf, send, recv, axis, copies):
    size = lax.axis_size(axis)
    me = lax.axis_index(axis)
    for copy in copies:
        copy.wait_send()
    for s in range(1, size):
        other = lax.rem(me + s, size)
        push(buf.at[other], buf.at[other], send.at[s - 1], recv.at[other], axis, other).wait_recv()


def pack_stats(sums, squares):
    rows = sums.shape[0]
    lane = lax.broadcasted_iota(jnp.int32, (rows, 128), 1)
    both = jnp.where(lane == 0, sums, jnp.where(lane == 1, squares, 0.0))
    return jnp.transpose(both)[:8]


def open_stats(total, width):
    rows = total.shape[1]
    tall = jnp.concatenate([total, jnp.zeros((120, rows), F32)], axis=0)
    back = jnp.transpose(tall)
    middle = back[:, 0:1] / width
    power = back[:, 1:2] / width
    return middle, lax.rsqrt(power - middle * middle + 1e-06)


def places(tmap, tlen, first, shape, dim):
    spot = lax.broadcasted_iota(jnp.int32, shape, dim)
    base = jnp.zeros(shape, jnp.int32)
    for j in range(shape[dim] // TILE):
        base = jnp.where(spot >= j * TILE, (tmap[first + j] - j) * TILE, base)
    where = spot + base
    image = where >= TXT
    return image, image | (where < tlen[0])


def row_keep(tmap, tlen, me, rows):
    _, valid = places(tmap, tlen, me * (rows // TILE), (rows, 1), 0)
    return jnp.where(valid, 1.0, 0.0)


def pick(z, values):
    out = values[-1]
    for i in range(len(values) - 2, -1, -1):
        out = jnp.where(z == i, values[i], out)
    return out


def front_kernel(
    tmap, tlen, hid, ss, qg, kg, w, q_out, k_out, v_out, act_out,
    xg, st, acc, wbuf, mod, xs, xr, ts, tr, ws,
):
    z = lax.axis_index("fsdp")
    rows, part = hid.shape
    width = part * 4
    span = q_out.shape[1]
    tiles = acc.shape[1] // span
    keep = row_keep(tmap, tlen, lax.axis_index("seq"), rows)
    order = [
        z,
        pick(z, [1, 0, 3, 2]),
        pick(z, [2, 2, 1, 1]),
        pick(z, [3, 3, 0, 0]),
    ]

    def wcopy(p):
        at = pl.multiple_of(order[p] * part, part)
        return pltpu.make_async_copy(w.at[pl.ds(at, part), :], wbuf.at[p], ws.at[p])

    for p in range(4):
        wcopy(p).start()
    greet(("fsdp",))
    xg[z] = hid[...]

    def hop(c, way):
        target = jnp.minimum(z + 1, 3) if way == 0 else jnp.maximum(z - 1, 0)
        return push(xg.at[c], xg.at[c], xs.at[way, c], xr.at[c], "fsdp", target)

    @pl.when(z < 3)
    def _():
        hop(z, 0).start()

    @pl.when(z > 0)
    def _():
        hop(z, 1).start()

    own = (hid[...].astype(F32)) * keep
    st[z] = pack_stats(
        jnp.sum(own, axis=1, keepdims=True), jnp.sum(own * own, axis=1, keepdims=True)
    )
    sent = spread(st, ts, tr, "fsdp")
    collect(st, ts, tr, "fsdp", sent)
    middle, inv = open_stats(st[0] + st[1] + st[2] + st[3], width)

    def arrive(c):
        hop(c, 0).wait_recv()

        @pl.when((c < z) & (z < 3))
        def _():
            hop(c, 0).start()

        @pl.when((c > z) & (z > 0))
        def _():
            hop(c, 1).start()

    inner = (z > 0) & (z < 3)
    for p in range(4):
        c = order[p]
        if p == 1:
            arrive(c)

            @pl.when(inner)
            def _():
                arrive(order[2])
        if p == 2:
            @pl.when(jnp.logical_not(inner))
            def _():
                arrive(order[2])
        if p == 3:
            arrive(c)
        vals = xg[c].astype(F32) * keep
        cut = pl.ds(pl.multiple_of(c * part, part), part)
        mod[...] = ((1.0 + ss[1:2, cut]) * ((vals - middle) * inv) + ss[0:1, cut]).astype(BF)
        wcopy(p).wait()

        def value(i):
            at = pl.ds(pl.multiple_of(i * span, span), span)
            return at, jnp.dot(mod[...], wbuf[p, :, at], preferred_element_type=F32)

        def tile(i, carry):
            at, got = value(i)
            if p == 0:
                acc[:, at] = got
            else:
                acc[:, at] += got
            return carry

        def last(i, carry):
            at, got = value(i)
            to = pl.ds(pl.multiple_of((i - 3) * span, span), span)
            act_out[:, to] = jax.nn.gelu(acc[:, at] + got, approximate=True).astype(BF)
            return carry

        if p < 3:
            lax.fori_loop(0, tiles, tile, 0)
        else:
            for i, gain, dst in ((1, kg, k_out), (2, None, v_out), (0, qg, q_out)):
                at, got = value(i)
                got = acc[:, at] + got
                if gain is None:
                    dst[...] = got.astype(BF)
                    continue
                for h in range(span // HD):
                    cols = slice(h * HD, (h + 1) * HD)
                    vals = got[:, cols]
                    scaled = vals * lax.rsqrt(
                        jnp.mean(vals * vals, axis=1, keepdims=True) + 1e-06
                    )
                    dst[:, cols] = (scaled * gain[...]).astype(BF)
            lax.fori_loop(3, tiles, last, 0)

    for c in range(4):
        @pl.when((z < 3) & (z >= c))
        def _():
            hop(c, 0).wait_send()

        @pl.when((z > 0) & (z <= c))
        def _():
            hop(c, 1).wait_send()


def vmem(count):
    return [pl.BlockSpec(memory_space=pltpu.VMEM)] * count


def smem(count):
    return [pl.BlockSpec(memory_space=pltpu.SMEM)] * count


def front(tmap, tlen, hid, ss, qg, kg, w, span):
    rows, part = hid.shape
    cols = w.shape[1]
    dma = pltpu.SemaphoreType.DMA
    shape = jax.ShapeDtypeStruct
    return pl.pallas_call(
        front_kernel,
        out_shape=(
            shape((rows, span), BF),
            shape((rows, span), BF),
            shape((rows, span), BF),
            shape((rows, cols - 3 * span), BF),
        ),
        in_specs=smem(2) + vmem(4) + [pl.BlockSpec(memory_space=pltpu.HBM)],
        out_specs=tuple(vmem(4)),
        scratch_shapes=[
            pltpu.VMEM((4, rows, part), BF),
            pltpu.VMEM((4, 8, rows), F32),
            pltpu.VMEM((rows, cols), F32),
            pltpu.VMEM((4, part, cols), BF),
            pltpu.VMEM((rows, part), BF),
            dma((2, 4)),
            dma((4,)),
            dma((3,)),
            dma((4,)),
            dma((4,)),
        ],
        compiler_params=pltpu.CompilerParams(
            collective_id=1, has_side_effects=True, vmem_limit_bytes=60 << 20
        ),
        cost_estimate=pl.CostEstimate(
            flops=2 * rows * 4 * part * cols, bytes_accessed=8 * part * cols, transcendentals=0
        ),
    )(tmap, tlen, hid, ss, qg, kg, w)


def back_kernel(
    tmap, tlen, guide, step, q, k, v, act, hid, md, head, lats, w,
    up_out, lat_out, norm_out, peak_out,
    kbuf, vbuf, high, low, gain, att, part, sbuf, rbuf, wbuf, st, vel, vsend, vrec, line, mix, swap, tot,
    ps, kq, vq, ss, rs, ws, ts, tr, us, ur, vs, vr, gs, gr, ks, kr,
):
    z = lax.axis_index("fsdp")
    g = lax.axis_index("guide")
    me = lax.axis_index("seq")
    rows, width = hid.shape
    tiles = rows // TILE
    cut = pl.ds(pl.multiple_of(z * width, width), width)
    keep = row_keep(tmap, tlen, me, rows)
    my_image, my_valid = places(tmap, tlen, me * tiles, (1, rows), 1)
    order = [
        pick(z, [3, 3, 0, 0]),
        pick(z, [2, 0, 3, 1]),
        pick(z, [1, 2, 1, 2]),
        z,
    ]

    def wcopy(p):
        at = pl.multiple_of(order[p] * width, width)
        return pltpu.make_async_copy(w.at[:, pl.ds(at, width)], wbuf.at[p], ws.at[p])

    for p in range(4):
        wcopy(p).start()
    kbuf[me] = k[...]
    vbuf[me] = v[...]
    greet(("fsdp", "seq", "guide"))
    near_x = me + 1 - 2 * lax.rem(me, 2)
    near_y = lax.rem(me + 2, 4)
    across = 3 - me

    def key_hop(src, at, target):
        return push(kbuf.at[src], kbuf.at[src], ps.at[at], kq.at[src], "seq", target)

    def value_hop(src, at, target):
        return push(vbuf.at[src], vbuf.at[src], ps.at[at], vq.at[src], "seq", target)

    moves = [
        key_hop(me, 0, near_x),
        value_hop(me, 1, near_y),
        key_hop(me, 2, near_y),
        value_hop(me, 3, near_x),
        key_hop(near_x, 4, near_y),
        value_hop(near_y, 5, near_x),
    ]
    for move in moves[:2]:
        move.start()

    span = q.shape[1]
    rate = HD ** (-0.5) * 1.4426950408889634

    def attend(src, first):
        _, open_keys = places(tmap, tlen, src * tiles, (1, rows), 1)

        def heads(i, carry):
            for j in range(2):
                h = i * 2 + j
                at = pl.ds(pl.multiple_of(h * HD, HD), HD)
                s = lax.dot_general(
                    q[:, at],
                    kbuf[src, :, at],
                    (((1,), (1,)), ((), ())),
                    preferred_element_type=F32,
                )
                s = jnp.where(open_keys, s, -1e30)
                top = jnp.max(s, axis=1, keepdims=True)
                if not first:
                    top = jnp.maximum(top, high[h])
                p = jnp.exp2((s - top) * rate)
                total = jnp.sum(p, axis=1, keepdims=True)
                got = jnp.dot(p.astype(BF), vbuf[src, :, at], preferred_element_type=F32)
                if not first:
                    shrink = jnp.exp2((high[h] - top) * rate)
                    total = total + low[h] * shrink
                    got = got + gain[:, at] * shrink
                high[h] = top
                low[h] = total
                gain[:, at] = got
            return carry

        lax.fori_loop(0, span // (2 * HD), heads, 0)

    def hop(d, way):
        target = jnp.minimum(z + 1, 3) if way == 0 else jnp.maximum(z - 1, 0)
        return push(sbuf.at[d], rbuf.at[way, d], ss.at[d], rs.at[way, d], "fsdp", target)

    ends = (z == 0) | (z == 3)
    attend(me, True)
    for p in range(4):
        d = order[p]
        wcopy(p).wait()

        def tile(i, carry):
            at = pl.ds(pl.multiple_of(i * 256, 256), 256)
            part[d, :, at] = jnp.dot(act[...], wbuf[p, span:, at], preferred_element_type=F32)
            return carry

        lax.fori_loop(0, width // 256, tile, 0)
        if p == 0:
            for move in moves[:2]:
                move.wait_send()
            for move in moves[2:4]:
                move.start()
            key_hop(near_x, 0, near_x).wait_recv()
            value_hop(near_y, 1, near_y).wait_recv()
    for move in moves[2:4]:
        move.wait_send()
    for move in moves[4:]:
        move.start()
    value_hop(near_x, 3, near_x).wait_recv()
    attend(near_x, False)
    key_hop(near_y, 2, near_y).wait_recv()
    attend(near_y, False)
    key_hop(across, 4, near_y).wait_recv()
    value_hop(across, 5, near_x).wait_recv()
    attend(across, False)
    for h in range(span // HD):
        at = slice(h * HD, (h + 1) * HD)
        att[:, at] = (gain[:, at] / low[h]).astype(BF)
    for p in range(4):
        d = order[p]

        def tile(i, carry):
            at = pl.ds(pl.multiple_of(i * 256, 256), 256)
            part[d, :, at] += jnp.dot(att[...], wbuf[p, :span, at], preferred_element_type=F32)
            return carry

        lax.fori_loop(0, width // 256, tile, 0)
        if p < 3:
            @pl.when(ends)
            def _():
                sbuf[d] = part[d].astype(BF)
                if p > 0:
                    hop(order[p - 1], 0).wait_send()

            @pl.when(z == 0)
            def _():
                hop(d, 0).start()

            @pl.when(z == 3)
            def _():
                hop(d, 1).start()

    def relay(d, way):
        hop(d, way).wait_recv()
        sbuf[d] = (part[d] + rbuf[way, d].astype(F32)).astype(BF)
        hop(d, way).start()

    @pl.when(z == 1)
    def _():
        relay(3, 0)
        relay(2, 0)
        relay(0, 1)

    @pl.when(z == 2)
    def _():
        relay(0, 1)
        relay(1, 1)
        relay(3, 0)

    mix[...] = part[z]

    @pl.when(z > 0)
    def _():
        hop(z, 0).wait_recv()
        mix[...] += rbuf[0, z].astype(F32)

    @pl.when(z < 3)
    def _():
        hop(z, 1).wait_recv()
        mix[...] += rbuf[1, z].astype(F32)

    x = hid[...].astype(F32) * keep
    up = ((x + md[2:3, cut] * mix[...]) * keep).astype(BF)
    up_out[...] = up
    wide = up.astype(F32)
    st[z] = pack_stats(
        jnp.sum(wide, axis=1, keepdims=True), jnp.sum(wide * wide, axis=1, keepdims=True)
    )
    stats_sent = spread(st, ts, tr, "fsdp")
    vpart = lax.dot_general(
        head[:, cut].astype(F32),
        wide * (1.0 + md[4:5, cut]),
        (((1,), (1,)), ((), ())),
        precision=lax.Precision.HIGHEST,
        preferred_element_type=F32,
    )
    share = vsend.shape[1]
    for d in range(4):
        vsend[d] = vpart[d * share : (d + 1) * share]

    def give(d, source, at):
        return push(vsend.at[d], vrec.at[source], us.at[at], ur.at[source], "fsdp", d)

    for s in range(1, 4):
        give(lax.rem(z + s, 4), z, s - 1).start()
    my_head = head[pl.ds(pl.multiple_of(z * share, share), share), :].astype(F32)
    scale_sum = jnp.sum(my_head * (1.0 + md[4:5, :]), axis=1, keepdims=True)
    shift_sum = jnp.sum(my_head * md[3:4, :], axis=1, keepdims=True)
    collect(st, ts, tr, "fsdp", stats_sent)
    total = st[0] + st[1] + st[2] + st[3]
    middle = total[0:1] / (width * 4)
    power = total[1:2] / (width * 4)
    inv = lax.rsqrt(power - middle * middle + 1e-06)
    mine = vsend[z]
    for s in range(1, 4):
        other = lax.rem(z + s, 4)
        give(other, other, s - 1).wait_recv()
        mine = mine + vrec[other]
    vel[z] = inv * (mine - middle * scale_sum) + shift_sum
    sent = spread(vel, vs, vr, "fsdp")
    collect(vel, vs, vr, "fsdp", sent)
    for d in range(4):
        line[d * share : (d + 1) * share, :] = vel[d]
    velocity = line[...]
    half = lats.shape[0] // 2
    other = 1 - g
    swap[0] = line[pl.ds(pl.multiple_of(other * half, half), half), :]
    cross = push(swap.at[0], swap.at[1], gs, gr, "guide", other)
    cross.start()
    full = jnp.sum(jnp.where(my_valid, total[1:2], 0.0), axis=1, keepdims=True)
    top = jnp.max(jnp.where(my_image, velocity, -jnp.inf), axis=1, keepdims=True)
    top = jnp.max(top, axis=0, keepdims=True)
    level = lax.broadcasted_iota(jnp.int32, (8, 128), 0)
    tot[me] = jnp.where(level == 0, full, top)
    sent = spread(tot, ks, kr, "seq")
    collect(tot, ks, kr, "seq", sent)
    added = tot[0] + tot[1] + tot[2] + tot[3]
    peak = jnp.maximum(jnp.maximum(tot[0], tot[1]), jnp.maximum(tot[2], tot[3]))
    count = (IMG + tlen[0]).astype(F32) * (width * 4)
    norm_out[...] = jnp.sqrt(added[0:1, 0:1] / count)
    peak_out[...] = peak[1:2, 0:1]
    cross.wait()
    own = line[pl.ds(pl.multiple_of(g * half, half), half), :]
    theirs = swap[1]
    cond = jnp.where(g == 0, own, theirs)
    free = jnp.where(g == 0, theirs, own)
    guided = free + guide[0] * (cond - free)
    mine = lats[pl.ds(pl.multiple_of(g * half, half), half), :]
    lat_out[...] = jnp.where(my_image, mine + step[0] * guided, 0.0)
    for move in moves[4:]:
        move.wait_send()
    for s in range(1, 4):
        give(lax.rem(z + s, 4), z, s - 1).wait_send()
    for d in range(4):
        @pl.when((z != d) & jnp.logical_not(ends))
        def _():
            hop(d, 0).wait_send()

    @pl.when(ends)
    def _():
        hop(order[2], 0).wait_send()


def back(tmap, tlen, guide, step, q, k, v, act, hid, md, head, lats, w):
    rows, width = hid.shape
    depth = w.shape[0]
    dma = pltpu.SemaphoreType.DMA
    shape = jax.ShapeDtypeStruct
    return pl.pallas_call(
        back_kernel,
        out_shape=(
            shape((rows, width), BF),
            shape((lats.shape[0] // 2, rows), F32),
            shape((1, 1), F32),
            shape((1, 1), F32),
        ),
        in_specs=smem(4) + vmem(8) + [pl.BlockSpec(memory_space=pltpu.HBM)],
        out_specs=tuple(vmem(4)),
        scratch_shapes=[
            pltpu.VMEM((4,) + k.shape, BF),
            pltpu.VMEM((4,) + k.shape, BF),
            pltpu.VMEM((k.shape[1] // HD, rows, 1), F32),
            pltpu.VMEM((k.shape[1] // HD, rows, 1), F32),
            pltpu.VMEM(q.shape, F32),
            pltpu.VMEM(q.shape, BF),
            pltpu.VMEM((4, rows, width), F32),
            pltpu.VMEM((4, rows, width), BF),
            pltpu.VMEM((2, 4, rows, width), BF),
            pltpu.VMEM((4, depth, width), BF),
            pltpu.VMEM((4, 8, rows), F32),
            pltpu.VMEM((4, lats.shape[0] // 4, rows), F32),
            pltpu.VMEM((4, lats.shape[0] // 4, rows), F32),
            pltpu.VMEM((4, lats.shape[0] // 4, rows), F32),
            pltpu.VMEM(lats.shape, F32),
            pltpu.VMEM((rows, width), F32),
            pltpu.VMEM((2, lats.shape[0] // 2, rows), F32),
            pltpu.VMEM((4, 8, 128), F32),
            dma((6,)),
            dma((4,)),
            dma((4,)),
            dma((4,)),
            dma((2, 4)),
            dma((4,)),
            dma((3,)),
            dma((4,)),
            dma((3,)),
            dma((4,)),
            dma((3,)),
            dma((4,)),
            dma,
            dma,
            dma((3,)),
            dma((4,)),
        ],
        compiler_params=pltpu.CompilerParams(
            collective_id=2, has_side_effects=True, vmem_limit_bytes=60 << 20
        ),
        cost_estimate=pl.CostEstimate(
            flops=8 * rows * depth * width, bytes_accessed=8 * depth * width, transcendentals=0
        ),
    )(tmap, tlen, guide, step, q, k, v, act, hid, md, head, lats, w)


def fast_shards(
    hidden,
    modulation,
    in_weight,
    query_gain,
    key_gain,
    out_weight,
    head_weight,
    latents,
    step_size,
    guidance,
    text_len,
    tile_map,
):
    whole_out = lax.all_gather(out_weight, "guide", axis=1, tiled=True)
    span = (in_weight.shape[1] - out_weight.shape[0]) // 2
    rows5 = modulation[0, 0]
    queries, keys, values, activated = front(
        tile_map, text_len, hidden[0], rows5, query_gain[None], key_gain[None], in_weight, span
    )
    updated, next_latents, norm, peak = back(
        tile_map, text_len, guidance, step_size, queries, keys, values, activated, hidden[0],
        rows5, head_weight.T, latents, whole_out,
    )
    return (updated[None], next_latents, norm, peak)


def solution(mesh):
    placed = (
        P("guide", "seq", "fsdp"),
        P("guide", None, None, None),
        P(None, "fsdp"),
        P(),
        P(),
        P("fsdp", "guide"),
        P(),
        P(None, "seq"),
        P(),
        P(),
        P(),
        P(),
    )
    shape = dict(mesh.shape)
    planned = shape["fsdp"] == 4 and shape["seq"] == 4 and shape["guide"] == 2

    def chosen(*args):
        return (fast_shards if planned and args[10].shape[0] == 1 else shards)(*args)

    return jax.shard_map(
        chosen,
        mesh=mesh,
        in_specs=placed,
        out_specs=(
            P("guide", "seq", "fsdp"),
            P("guide", "seq"),
            P("guide", None),
            P("guide", None),
        ),
        check_vma=False,
    )
```
